128 devices in a mesh: pipe: 4 (over x_hi, core), dp: 32 (over y, z, x_lo).
Axes of the slice: x: 4 (x_hi: 2, x_lo: 2; x = x_hi * 2 + x_lo), y: 4, z: 4, core: 2. Of those that a mesh axis runs over, the one named last changes fastest.
Arguments:
- layer_input: bfloat16 [4, 4096, 8192], P('pipe', 'dp'), may hold values from -130 to 130
- queries: bfloat16 [4, 4096, 4096], P('pipe', 'dp'), may hold values from -35 to 35
- out_grad: bfloat16 [4, 4096, 4096], P('pipe', 'dp'), may hold values from -6 to 6
- top_grad: bfloat16 [4096, 8192], P('dp'), may hold values from -4 to 4
- norm_gain: bfloat16 [4, 8192], P('pipe', 'dp'), may hold values from 0.5 to 1.5
- key_weight: bfloat16 [4, 8192, 512], P('pipe', 'dp'), may hold values from -0.0625 to 0.0625
- value_weight: bfloat16 [4, 8192, 512], P('pipe', 'dp'), may hold values from -0.0625 to 0.0625
- weight_exponents: int32 [4, 2, 64, 4], P('pipe', None, 'dp'), may hold values from -1 to 1
- doc_lengths: int32 [64], replicated, may hold values from 1 to 512, 4096 in all
Outputs:
- input_grad: bfloat16 [4, 4096, 8192], P('pipe', 'dp')
- query_grad: bfloat16 [4, 4096, 4096], P('pipe', 'dp')
- key_weight_grad: float32 [4, 8192, 512], P('pipe', 'dp')
- value_weight_grad: float32 [4, 8192, 512], P('pipe', 'dp')
- gain_grad: float32 [4, 8192], P('pipe', 'dp')
The draws below stay inside these ranges and needn't reach their ends.
Inputs may be any that keep to these rules, and one draw needn't show every extreme that they name: `doc_lengths`: the lengths sum to 4096; the longest is exactly 512. `weight_exponents`: one exponent of two for each 128 x 128 block.
All inputs are finite; a program needn't handle non-finite values.
Results may differ from the reference program's by a relative error of at most 0.035.
The reference program's roundings to bfloat16 on the way (of `hidden`, `probs_low` and `score_grads`) count: a program that leaves them out, or rounds other values in their place, can miss the bound.
Values may be sent and summed in bfloat16 or wider, within the bound.
A program may use at most 192 MiB of HBM per device.

```python
import math
import jax
import jax.numpy as jnp
import numpy as np
from jax import lax

D = 8192
KV_HEADS = 4
Q_PER_KV = 8
HEAD = 128
BLOCK = 128
REACH = 4
TOK_DEV = 128
SECTIONS = 4
KVW = 512
QW = 4096
SEQ = 4096
MOST_DOC = 512
NDOCS = 64
N_DP = 32


def log_scales(key, shape_dims, top_value):
    return jnp.exp(jax.random.uniform(key, shape_dims, jnp.float32, 0.0, jnp.log(top_value)))


def draw_layer_input(key, part):
    subkeys = jax.random.split(jax.random.fold_in(key, 11), 3)
    shape_dims = (SECTIONS, SEQ, D)
    base_draw = jnp.clip(jax.random.normal(subkeys[0], shape_dims, jnp.float32), -5.0, 5.0)
    top_value = 10.0
    row_scale = log_scales(subkeys[1], (SECTIONS, SEQ, 1), top_value)
    col_scale = log_scales(subkeys[2], (SECTIONS, 1, D), top_value)
    return (base_draw * row_scale * col_scale * 0.25).astype(jnp.bfloat16)


def draw_queries(key, part):
    subkeys = jax.random.split(jax.random.fold_in(key, 23), 1)
    shape_dims = (SECTIONS, SEQ, QW)
    scaled = jnp.clip(jax.random.normal(subkeys[0], shape_dims, jnp.float32), -5.0, 5.0)
    return scaled.astype(jnp.bfloat16)


def plant(entries, own_key, low, largest):
    longest = entries.shape.index(max(entries.shape))
    spots = []
    for shift in (0, 1):
        where = [jax.random.randint(jax.random.fold_in(own_key, axis), (), 0, length) for axis, length in enumerate(entries.shape)]
        where[longest] = (where[longest] + shift) % entries.shape[longest]
        spots.append(tuple(where))
    return entries.at[spots[0]].set(low).at[spots[1]].set(largest)


def shard_levels(stream_key, extent, pieces, low, high):
    level = 1.0
    for position, parts in pieces:
        heights = jax.random.uniform(jax.random.fold_in(jax.random.fold_in(stream_key, 6), position), (parts,), jnp.float32, low / len(pieces), high / len(pieces))
        level = level * jnp.repeat(jnp.exp(heights), extent[position] // parts).reshape((-1,) + (1,) * (len(extent) - 1 - position))
    return level


def length_profile(number_of, total, most, lean):
    portions = [(1 << 20) // math.isqrt(rank ** lean) + 1 for rank in range(2, number_of + 1)]
    spare, holding = total - most - (number_of - 1), [1] * (number_of - 1)
    while spare > 0:
        free = [i for i in range(number_of - 1) if holding[i] < most]
        whole, budget = sum([portions[i] for i in free]), spare
        for i in free:
            more = min(most - holding[i], max(1, budget * portions[i] // whole), spare)
            holding[i] = holding[i] + more
            spare = spare - more
    return np.array([most] + holding)


def uneven(stream_key, count, total, most, slope):
    if count == 2:
        one = jax.random.randint(stream_key, (), max(1, total - most), min(most, total - 1) + 1)
        return jnp.stack([one, total - one])
    lengths = jnp.asarray(length_profile(count, total, most, slope), jnp.int32)
    twos = (count - 1) // 2
    giver, taker = lengths[1:1 + 2 * twos:2], lengths[2:2 + 2 * twos:2]
    margin = jnp.minimum(giver - 1, most - taker)
    passed = jax.random.randint(jax.random.fold_in(stream_key, 1), (twos,), 0, 1 << 20) % (margin + 1)
    lengths = lengths.at[1:1 + 2 * twos:2].set(giver - passed).at[2:2 + 2 * twos:2].set(taker + passed)
    return lengths[jax.random.permutation(jax.random.fold_in(stream_key, 2), count)]


def scatter_about(stream_key, extent, spread, bound, cuts=(), held_as=jnp.bfloat16):
    values = spread * jax.random.normal(stream_key, extent, jnp.float32)
    if cuts:
        values = values * shard_levels(stream_key, extent, cuts, -0.22, 0.18)
    return jnp.clip(values, -bound, bound).astype(held_as)


def setup_inputs(seed: int = 0) -> dict:
    splits = jax.random.split(jax.random.key(seed), 10)
    return {
        "layer_input": draw_layer_input(jax.random.fold_in(splits[9], 71), 0),
        "queries": draw_queries(jax.random.fold_in(splits[9], 71), 0),
        "out_grad": scatter_about(splits[2], (SECTIONS, SEQ, QW), 1.0, 6.0, ((0, 4), (1, 32))),
        "top_grad": scatter_about(splits[3], (SEQ, D), 0.3, 4.0, ((0, 32),)),
        "norm_gain": jnp.clip(1.0 + 0.1 * jax.random.normal(splits[4], (SECTIONS, D), jnp.float32), 0.5, 1.5).astype(jnp.bfloat16),
        "key_weight": scatter_about(splits[5], (SECTIONS, D, KVW), D ** -0.5, 0.0625, ((0, 4), (1, 32))),
        "value_weight": scatter_about(splits[6], (SECTIONS, D, KVW), D ** -0.5, 0.0625, ((0, 4), (1, 32))),
        "weight_exponents": plant(jax.random.randint(splits[7], (SECTIONS, 2, D // BLOCK, KVW // BLOCK), -1, 2), jax.random.fold_in(splits[7], 1), -1, 1).astype(jnp.int32),
        "doc_lengths": uneven(splits[8], NDOCS, SEQ, MOST_DOC, 2).astype(jnp.int32),
    }


theta_base = 500000.0
eps_norm = 1e-05
masked_score = -1e+30

def rotary_tables(positions, head_size):
    half_size = head_size // 2
    frequency = theta_base ** (-(jnp.arange(half_size).astype(jnp.float32) * 2.0 / head_size))
    angles = positions.astype(jnp.float32)[:, None] * frequency[None, :]
    return (jnp.cos(angles)[:, None, :], jnp.sin(angles)[:, None, :])

def rotate(values, cosine, sine):
    half_size = values.shape[-1] // 2
    first = values[..., :half_size]
    second = values[..., half_size:]
    return jnp.concatenate([first * cosine - second * sine, second * cosine + first * sine], axis=-1)

def unrotate(grads, cosine, sine):
    half_size = grads.shape[-1] // 2
    first = grads[..., :half_size]
    second = grads[..., half_size:]
    return jnp.concatenate([first * cosine + second * sine, second * cosine - first * sine], axis=-1)

def doc_info(token_index, doc_lengths):
    starts = (jnp.cumsum(doc_lengths) - doc_lengths).astype(jnp.int32)
    before = starts[None, :] <= token_index[:, None]
    doc_number = (lax.optimization_barrier(jnp.sum(before.astype(jnp.int32), axis=1)) - 1).astype(jnp.int32)
    doc_start = lax.optimization_barrier(jnp.max(jnp.where(before, starts[None, :], 0), axis=1)).astype(jnp.int32)
    return (doc_number, (token_index - doc_start).astype(jnp.int32))

def dequantize(values, exponents, block_side):
    row_blocks, col_blocks = exponents.shape
    factors = jnp.exp2(exponents.astype(jnp.float32))
    shaped = values.astype(jnp.float32).reshape(row_blocks, block_side, col_blocks, block_side)
    return (shaped * factors[:, None, :, None]).reshape(values.shape).astype(jnp.bfloat16)

def to_low(values):
    return lax.optimization_barrier(values.astype(jnp.bfloat16)).astype(jnp.float32)

def section_backward(inputs_low, query_all, grad_all, gain, key_weight, value_weight, exponents, doc_number, positions):
    key_full = dequantize(key_weight, exponents[0], BLOCK)
    value_full = dequantize(value_weight, exponents[1], BLOCK)
    inputs = inputs_low.astype(jnp.float32)
    root_mean = jnp.sqrt(lax.optimization_barrier(jnp.mean(inputs * inputs, axis=1, keepdims=True)) + eps_norm)
    normed = inputs / root_mean
    gain_f = gain.astype(jnp.float32)
    hidden = (normed * gain_f).astype(jnp.bfloat16)
    cosine, sine = rotary_tables(positions, HEAD)
    key_proj = jnp.dot(hidden, key_full, preferred_element_type=jnp.float32).reshape(SEQ, KV_HEADS, HEAD)
    keys = rotate(key_proj, cosine, sine).astype(jnp.bfloat16)
    values = jnp.dot(hidden, value_full, preferred_element_type=jnp.float32).astype(jnp.bfloat16).reshape(SEQ, KV_HEADS, HEAD)
    pad_rows = REACH * TOK_DEV
    window = (REACH + 1) * TOK_DEV
    key_pad = jnp.concatenate([jnp.zeros((pad_rows, KV_HEADS, HEAD), jnp.bfloat16), keys]).astype(jnp.float32)
    value_pad = jnp.concatenate([jnp.zeros((pad_rows, KV_HEADS, HEAD), jnp.bfloat16), values]).astype(jnp.float32)
    doc_pad = jnp.concatenate([jnp.full((pad_rows,), -1, jnp.int32), doc_number.astype(jnp.int32)])
    index_pad = (jnp.arange(SEQ + pad_rows) - pad_rows).astype(jnp.int32)
    queries_f = query_all.astype(jnp.float32).reshape(SEQ, KV_HEADS, Q_PER_KV, HEAD)
    grads_f = grad_all.astype(jnp.float32).reshape(SEQ, KV_HEADS, Q_PER_KV, HEAD)
    inv_root = 1.0 / jnp.sqrt(jnp.float32(HEAD))

    def one_block(carry, block_number):
        key_acc, value_acc = carry
        row_start = (block_number * TOK_DEV).astype(jnp.int32)
        query_rows = lax.dynamic_slice_in_dim(queries_f, row_start, TOK_DEV, 0)
        grad_rows = lax.dynamic_slice_in_dim(grads_f, row_start, TOK_DEV, 0)
        query_doc = lax.dynamic_slice_in_dim(doc_number.astype(jnp.int32), row_start, TOK_DEV, 0)
        query_index = (row_start + jnp.arange(TOK_DEV)).astype(jnp.int32)
        key_rows = lax.dynamic_slice_in_dim(key_pad, row_start, window, 0)
        value_rows = lax.dynamic_slice_in_dim(value_pad, row_start, window, 0)
        key_doc = lax.dynamic_slice_in_dim(doc_pad, row_start, window, 0)
        key_index = lax.dynamic_slice_in_dim(index_pad, row_start, window, 0)
        visible = (key_index[None, :] >= 0) & (key_doc[None, :] == query_doc[:, None]) & (key_index[None, :] <= query_index[:, None])
        raw_scores = jnp.einsum('qkgd,tkd->kgqt', query_rows, key_rows)
        scores = jnp.where(visible[None, None], raw_scores * inv_root, masked_score)
        row_max = lax.optimization_barrier(jnp.max(scores, axis=3, keepdims=True))
        exp_scores = jnp.exp(scores - row_max)
        softmax_out = exp_scores / lax.optimization_barrier(jnp.sum(exp_scores, axis=3, keepdims=True))
        probs_low = to_low(softmax_out)
        attended = jnp.einsum('kgqt,tkd->qkgd', probs_low, value_rows)
        out_dot = jnp.transpose(lax.optimization_barrier(jnp.sum(grad_rows * attended, axis=3)), (1, 2, 0))[..., None]
        value_term = jnp.einsum('kgqt,qkgd->tkd', probs_low, grad_rows)
        prob_grad = jnp.einsum('qkgd,tkd->kgqt', grad_rows, value_rows)
        score_grads = to_low(softmax_out * (prob_grad - out_dot))
        query_block = (jnp.einsum('kgqt,tkd->qkgd', score_grads, key_rows) * inv_root).astype(jnp.bfloat16).reshape(TOK_DEV, -1)
        key_term = to_low(jnp.einsum('kgqt,qkgd->tkd', score_grads, query_rows) * inv_root)
        value_term = to_low(value_term)
        key_acc = lax.dynamic_update_slice_in_dim(key_acc, lax.dynamic_slice_in_dim(key_acc, row_start, window, 0) + key_term, row_start, 0)
        value_acc = lax.dynamic_update_slice_in_dim(value_acc, lax.dynamic_slice_in_dim(value_acc, row_start, window, 0) + value_term, row_start, 0)
        return ((key_acc, value_acc), query_block)
    zero_acc = jnp.zeros((SEQ + pad_rows, KV_HEADS, HEAD), jnp.float32)
    (key_acc, value_acc), query_blocks = lax.scan(one_block, (zero_acc, zero_acc), jnp.arange(SEQ // TOK_DEV).astype(jnp.int32))
    query_grad = query_blocks.reshape(SEQ, -1)
    key_grads = unrotate(key_acc[pad_rows:], cosine, sine).astype(jnp.bfloat16).reshape(SEQ, -1)
    value_grads = value_acc[pad_rows:].astype(jnp.bfloat16).reshape(SEQ, -1)
    hidden_grad = jnp.dot(key_grads, key_full.T, preferred_element_type=jnp.float32) + jnp.dot(value_grads, value_full.T, preferred_element_type=jnp.float32)
    scaled_grad = hidden_grad * gain_f
    branch = (scaled_grad - normed * lax.optimization_barrier(jnp.mean(scaled_grad * normed, axis=1, keepdims=True))) / root_mean
    gain_terms = to_low(lax.optimization_barrier(jnp.sum((hidden_grad * normed).reshape(N_DP, TOK_DEV, D), axis=1)))
    gain_grad = lax.optimization_barrier(jnp.sum(gain_terms, axis=0))

    def weight_block(carry, block_number):
        key_total, value_total = carry
        row_start = (block_number * TOK_DEV).astype(jnp.int32)
        hidden_rows = lax.dynamic_slice_in_dim(hidden, row_start, TOK_DEV, 0)
        key_rows = lax.dynamic_slice_in_dim(key_grads, row_start, TOK_DEV, 0)
        value_rows = lax.dynamic_slice_in_dim(value_grads, row_start, TOK_DEV, 0)
        key_total = key_total + to_low(jnp.dot(hidden_rows.T, key_rows, preferred_element_type=jnp.float32))
        value_total = value_total + to_low(jnp.dot(hidden_rows.T, value_rows, preferred_element_type=jnp.float32))
        return ((key_total, value_total), None)
    zero_weight = jnp.zeros((D, KVW), jnp.float32)
    (key_wgrad, value_wgrad), unused = lax.scan(weight_block, (zero_weight, zero_weight), jnp.arange(N_DP).astype(jnp.int32))
    return (branch, query_grad, key_wgrad, value_wgrad, gain_grad)

def reference(layer_input, queries, out_grad, top_grad, norm_gain, key_weight, value_weight, weight_exponents, doc_lengths):
    token_index = jnp.arange(SEQ).astype(jnp.int32)
    doc_number, positions = doc_info(token_index, doc_lengths.astype(jnp.int32))
    carried = top_grad
    input_list = [None] * SECTIONS
    query_list = [None] * SECTIONS
    key_list = [None] * SECTIONS
    value_list = [None] * SECTIONS
    gain_list = [None] * SECTIONS
    for section_number in reversed(range(SECTIONS)):
        branch, query_grad, key_wgrad, value_wgrad, gain_grad = section_backward(layer_input[section_number], queries[section_number], out_grad[section_number], norm_gain[section_number], key_weight[section_number], value_weight[section_number], weight_exponents[section_number], doc_number, positions)
        carried = (carried.astype(jnp.float32) + branch).astype(jnp.bfloat16)
        input_list[section_number] = carried
        query_list[section_number] = query_grad
        key_list[section_number] = key_wgrad
        value_list[section_number] = value_wgrad
        gain_list[section_number] = gain_grad
    return (jnp.stack(input_list), jnp.stack(query_list), jnp.stack(key_list), jnp.stack(value_list), jnp.stack(gain_list))
```

```python
import functools
import math

import jax
import jax.numpy as jnp
import numpy as np
from jax import lax
from jax.experimental import pallas as pl
from jax.experimental.pallas import tpu as pltpu
from jax.sharding import PartitionSpec as P

D = 8192
KV_HEADS = 4
Q_PER_KV = 8
HEAD = 128
TOK = 128
REACH = 4
KVW = 512
QW = 4096
ROWS = 256
THETA = 500000.0
EPS = 1e-05
MASKED = -1e30

F = 8
T = 4
SLAB = 1024
WIN = (REACH + 1) * TOK
CHUNKS = 8
PAIR = 2

MESH = pl.DeviceIdType.MESH
NT = (((1,), (1,)), ((), ()))
NN = (((1,), (0,)), ((), ()))


def rows(start, size):
    return pl.ds(pl.multiple_of(start, size), size)


def cols(start, size):
    return pl.ds(pl.multiple_of(start, size), size)


def dot(a, b, dims=NN):
    return lax.dot_general(a, b, dims, preferred_element_type=jnp.float32)


def wide(col, width):
    return jnp.concatenate([col] * (width // col.shape[1]), axis=1)


def kernel(
    fac, docs, freq, x, q, do, top, gain, kw, vw,
    o_in, o_q, o_kw, o_vw, o_gain,
    xs, xr, kwv, vwv, wr, gr, rr, rown, qs, dos, cin, cout, cosb, sinb, bias,
    hbuf, ht, psend, precv, kwin, pt, dst, tb, ra, dq, gall, hgs, sgr, ab, bb,
    ws, wrecv, wown, gs, grecv, gacc,
    lsem, sx, rx, sr, rrs, sw, rw, sg, rg, sp, rp, skv, rkv, sb, rb,
    sga, rga, sh, rh, sws, rws, sgs, rgs, src_, rrc, osem,
):
    p = lax.axis_index("pipe")
    i = lax.axis_index("dp")
    f = i % F
    t = i // F
    xl = i % 2

    def slab(k, size=TOK):
        return slice(k * size, (k + 1) * size)

    def f_up(k):
        return (p, t * F + (f + k) % F)

    def f_down(k):
        return (p, t * F + (f + F - k) % F)

    def t_up(k):
        return (p, (t + k) % T * F + f)

    def t_down(k):
        return (p, (t + T - k) % T * F + f)

    def rcopy(src, dst, ssem, rsem, dev):
        return pltpu.make_async_remote_copy(
            src_ref=src, dst_ref=dst, send_sem=ssem, recv_sem=rsem,
            device_id=dev, device_id_type=MESH)

    def x_cols(n):
        return cols(((t + T - n % T) % T * F + (f + n // T) % F) * ROWS, ROWS)

    def load_x(n, carry):
        pltpu.make_async_copy(x.at[0, :, x_cols(n)], xs.at[n], lsem.at[0]).start()
        return carry

    lax.fori_loop(0, F * T, load_x, 0)
    pltpu.make_async_copy(kw.at[0], kwv, lsem.at[1]).start()
    pltpu.make_async_copy(vw.at[0], vwv, lsem.at[2]).start()

    def load_q(n, carry):
        pltpu.make_async_copy(
            q.at[0, :, cols(n * HEAD, HEAD)], qs.at[rows(n * TOK, TOK)], lsem.at[3]).start()
        pltpu.make_async_copy(
            do.at[0, :, cols(n * HEAD, HEAD)], dos.at[rows(n * TOK, TOK)], lsem.at[4]).start()
        return carry

    lax.fori_loop(0, KV_HEADS * Q_PER_KV, load_q, 0)

    @pl.when(p == 3)
    def _():
        def load_top(n, carry):
            pltpu.make_async_copy(top.at[:, x_cols(n)], cin.at[n], lsem.at[5]).start()
            return carry

        lax.fori_loop(0, F * T, load_top, 0)

    barrier = pltpu.get_barrier_semaphore()
    peers = [f_up(k) for k in range(1, F)] + [t_up(k) for k in range(1, T)]
    peers += [(p, (i + 2) % 32), (p, (i + 30) % 32)]
    peers += [((p + 1) % 4, i), ((p + 3) % 4, i)]
    for peer in peers:
        pl.semaphore_signal(barrier, inc=1, device_id=peer, device_id_type=MESH)
    pl.semaphore_wait(barrier, len(peers))

    pltpu.make_async_copy(xs, xs, lsem.at[0]).wait()

    def x_copy(k):
        return rcopy(xs.at[slab(k, T)], xr.at[slab(k, T)], sx.at[k], rx.at[k], f_up(k))

    for k in range(1, F):
        x_copy(k).start()
    xr[0:T] = xs[0:T]

    pltpu.make_async_copy(kw.at[0], kwv, lsem.at[1]).wait()
    pltpu.make_async_copy(vw.at[0], vwv, lsem.at[2]).wait()
    for rblock in range(2):
        for cblock in range(4):
            for which, wv in ((0, kwv), (1, vwv)):
                block = wv[slab(rblock), slab(cblock)].astype(jnp.float32)
                scaled = block * fac[which * 8 + rblock * 4 + cblock]
                wr[slab(rblock), slab(which * 4 + cblock)] = scaled.astype(jnp.bfloat16)
    gr[0:8, :] = jnp.broadcast_to(gain[...].astype(jnp.float32), (8, ROWS))

    def w_copy(k):
        return rcopy(wr.at[0:ROWS], wr.at[slab(k, ROWS)], sw.at[k], rw.at[k], t_up(k))

    def g_copy(k):
        return rcopy(gr.at[0:8], gr.at[slab(k, 8)], sg.at[k], rg.at[k], t_up(k))

    for k in range(1, T):
        w_copy(k).start()
        g_copy(k).start()

    def add_squares(n, acc):
        part = xs[n].astype(jnp.float32)
        part = part * part
        for c in range(ROWS // 128):
            acc = acc + part[:, slab(c)]
        return acc

    squares = lax.fori_loop(0, F * T, add_squares, jnp.zeros((TOK, 128), jnp.float32))
    mean_sq = jnp.sum(squares, axis=1, keepdims=True) * (1.0 / D)
    rinv = jnp.broadcast_to(1.0 / jnp.sqrt(mean_sq + EPS), (TOK, 128))
    rown[...] = rinv
    rr[0:8, :] = rinv.T[0:8, :]

    def r_copy(k):
        return rcopy(rr.at[0:8], rr.at[slab(k, 8)], sr.at[k], rrs.at[k], f_up(k))

    for k in range(1, F):
        r_copy(k).start()

    tok_col = i * TOK + lax.broadcasted_iota(jnp.int32, (TOK, 128), 0)
    tok_row = i * TOK + lax.broadcasted_iota(jnp.int32, (8, 128), 1)

    def scan_docs(n, carry):
        start, scol, srow = carry
        scol = jnp.where(start <= tok_col, start, scol)
        srow = jnp.where(start <= tok_row, start, srow)
        return start + docs[n], scol, srow

    _, scol, srow = lax.fori_loop(
        0, 64, scan_docs,
        (jnp.int32(0), jnp.zeros((TOK, 128), jnp.int32), jnp.zeros((8, 128), jnp.int32)))
    angle = (tok_col - scol).astype(jnp.float32) * freq[0:1, :]
    lane = lax.broadcasted_iota(jnp.int32, (TOK, 128), 1)
    sine = jnp.sin(angle)
    cosb[...] = jnp.cos(angle)
    sinb[...] = jnp.where(lane < 64, -sine, sine)
    key_index = (i - REACH) * TOK + lax.broadcasted_iota(jnp.int32, (WIN, 128), 0)
    seen = (key_index >= srow[0:1, :]) & (key_index <= tok_row[0:1, :])
    bias[...] = jnp.where(seen, 0.0, MASKED)

    for k in range(1, T):
        w_copy(k).wait_recv()
        g_copy(k).wait_recv()

    def inv_rms(k):
        return jnp.broadcast_to(rr[k * 8:k * 8 + 1, :], (TOK, 128)).T

    def slab_x(k):
        return jnp.concatenate(
            [xr[k * T + n].astype(jnp.float32) for n in range(T)], axis=1)

    gain_row = jnp.concatenate([gr[n * 8:n * 8 + 1, :] for n in range(T)], axis=1)

    def p_copy(k):
        return rcopy(psend.at[slab(k)], precv.at[slab(k)], sp.at[k], rp.at[k], f_down(k))

    for k in range(F):
        if k > 0:
            x_copy(k).wait_recv()
            r_copy(k).wait_recv()
        hidden = (slab_x(k) * wide(inv_rms(k), SLAB) * gain_row).astype(jnp.bfloat16)
        hbuf[slab(k), :] = hidden
        part = dot(hidden, wr[...]).astype(jnp.bfloat16)
        if k > 0:
            psend[slab(k), :] = part
            p_copy(k).start()
        else:
            precv[slab(k), :] = part

    for k in range(F):
        ht[:, slab(k)] = hbuf[slab(k), :].T

    for k in range(1, F):
        p_copy(k).wait_recv()

    def rope(block, sign):
        return block * cosb[...] + pltpu.roll(block, 64, 1) * (sinb[...] * sign)

    for c in range(8):
        total = precv[0:TOK, slab(c)].astype(jnp.float32)
        for k in range(1, F):
            total = total + precv[slab(k), slab(c)].astype(jnp.float32)
        if c < 4:
            total = rope(total, 1.0)
        kwin[REACH * TOK:, slab(c)] = total.astype(jnp.bfloat16)

    partner = (p, i + 1 - 2 * xl)
    ahead = (p, (i + 2) % 32)
    back = (p, (i + 30) % 32)

    def kv_copy(src, dst_slot, n, dev):
        return rcopy(kwin.at[slab(src)], kwin.at[slab(dst_slot)], skv.at[n], rkv.at[n], dev)

    hop1 = kv_copy(4, 2, 0, ahead)
    hop2 = kv_copy(2, 0, 1, ahead)
    even1 = kv_copy(4, 3, 2, partner)
    even2 = kv_copy(2, 1, 3, partner)
    odd1 = kv_copy(2, 3, 2, partner)
    odd2 = kv_copy(0, 1, 3, partner)
    hop1.start()

    @pl.when(xl == 0)
    def _():
        even1.start()

    hop1.wait_recv()
    hop2.start()

    @pl.when(xl == 0)
    def _():
        even2.start()

    @pl.when(xl == 1)
    def _():
        odd1.start()

    hop2.wait_recv()

    @pl.when(xl == 1)
    def _():
        odd2.start()

    pltpu.make_async_copy(qs, qs, lsem.at[3]).wait()
    pltpu.make_async_copy(dos, dos, lsem.at[4]).wait()
    even1.wait_recv()
    even2.wait_recv()

    inv_root = 1.0 / math.sqrt(HEAD)

    def one_kv_head(h, carry):
        kcol = cols(h * HEAD, HEAD)
        vcol = cols(KVW + h * HEAD, HEAD)
        keys = kwin[:, kcol]
        vals = kwin[:, vcol]
        keys_t = keys.T

        def heads(g, carry2):
            width = PAIR * TOK
            qrow = rows((h * Q_PER_KV + g * PAIR) * TOK, width)
            scores = dot(keys, qs[qrow, :], NT) * inv_root + wide(bias[...], width)
            top_score = jnp.max(scores, axis=0, keepdims=True)
            expd = jnp.exp(scores - top_score)
            probs = expd * (1.0 / jnp.sum(expd, axis=0, keepdims=True))
            low = probs.astype(jnp.bfloat16)
            pgrad = dot(vals, dos[qrow, :], NT)
            delta = jnp.sum(low.astype(jnp.float32) * pgrad, axis=0, keepdims=True)
            sgrad = (probs * (pgrad - delta)).astype(jnp.bfloat16)
            pcol = cols(g * width, width)
            pt[:, pcol] = low
            dst[:, pcol] = sgrad
            dqt = dot(keys_t, sgrad) * inv_root
            for n in range(PAIR):
                head = (h * Q_PER_KV + g * PAIR + n) * HEAD
                dq[:, cols(head, HEAD)] = dqt[:, slab(n)].T.astype(jnp.bfloat16)
            return carry2

        lax.fori_loop(0, Q_PER_KV // PAIR, heads, 0)
        hrow = rows(h * Q_PER_KV * TOK, Q_PER_KV * TOK)
        tb[:, vcol] = dot(pt[...], dos[hrow, :]).astype(jnp.bfloat16)
        tb[:, kcol] = (dot(dst[...], qs[hrow, :]) * inv_root).astype(jnp.bfloat16)
        return carry

    lax.fori_loop(0, KV_HEADS, one_kv_head, 0)

    def t_copy(src, n, dev):
        return rcopy(tb.at[slab(src)], ra.at[slab(n)], sb.at[n], rb.at[n], dev)

    back_a = t_copy(3, 0, partner)
    back_b = t_copy(1, 1, partner)
    back_c = t_copy(0, 2, back)
    back_d = t_copy(2, 3, back)
    back_b.start()
    back_a.start()

    def fold(s, n):
        tb[slab(s), :] = (tb[slab(s), :].astype(jnp.float32)
                          + ra[slab(n), :].astype(jnp.float32)).astype(jnp.bfloat16)

    back_b.wait_recv()

    @pl.when(xl == 1)
    def _():
        fold(0, 1)

    back_c.start()
    back_a.wait_recv()

    @pl.when(xl == 1)
    def _():
        fold(2, 0)

    @pl.when(xl == 0)
    def _():
        fold(2, 1)
        fold(4, 0)

    back_c.wait_recv()
    fold(2, 2)
    back_d.start()
    out_q = pltpu.make_async_copy(dq, o_q.at[0], osem.at[0])
    out_q.start()
    back_d.wait_recv()
    for c in range(8):
        total = (tb[slab(REACH), slab(c)].astype(jnp.float32)
                 + ra[slab(3), slab(c)].astype(jnp.float32))
        if c < 4:
            total = rope(total, -1.0)
        gall[0:TOK, slab(c)] = total.astype(jnp.bfloat16)

    def ga_copy(k):
        return rcopy(gall.at[0:TOK], gall.at[slab(k)], sga.at[k], rga.at[k], f_up(k))

    for k in range(1, F):
        ga_copy(k).start()

    gacc[...] = jnp.zeros_like(gacc)

    def h_copy(k):
        return rcopy(hgs.at[slab(k)], sgr.at[slab(k)], sh.at[k], rh.at[k], f_down(k))

    for k in range(F):
        if k > 0:
            ga_copy(k).wait_recv()
        hg = dot(gall[slab(k), :], wr[...], NT)
        scaled = (hg * gain_row).astype(jnp.bfloat16)
        if k > 0:
            hgs[slab(k), :] = scaled
            h_copy(k).start()
        else:
            sgr[slab(k), :] = scaled
        prod = hg * slab_x(k) * wide(inv_rms(k), SLAB)
        part = prod[0:8, :]
        for n in range(1, TOK // 8):
            part = part + prod[slab(n, 8), :]
        gacc[...] = gacc[...] + part

    gterm = jnp.broadcast_to(jnp.sum(gacc[...], axis=0, keepdims=True), (8, SLAB))
    for k in range(T):
        gs[slab(k, 8), :] = gterm[:, slab(k, ROWS)]

    def gs_copy(k):
        return rcopy(gs.at[slab(k, 8)], grecv.at[slab(k, 8)], sgs.at[k], rgs.at[k], t_down(k))

    def ws_copy(k):
        return rcopy(ws.at[slab(k, ROWS)], wrecv.at[slab(k, ROWS)], sws.at[k], rws.at[k],
                     t_down(k))

    for k in range(1, T):
        ws[slab(k, ROWS), :] = dot(ht[slab(k, ROWS), :], gall[...]).astype(jnp.bfloat16)
        ws_copy(k).start()
        gs_copy(k).start()
    wown[...] = dot(ht[0:ROWS, :], gall[...])

    dots = jnp.zeros((TOK, 128), jnp.float32)
    for k in range(F):
        if k > 0:
            h_copy(k).wait_recv()
        for c in range(SLAB // 128):
            dots = dots + (sgr[slab(k), slab(c)].astype(jnp.float32)
                           * xs[k * T + c // 2, :, slab(c % 2)].astype(jnp.float32))
    rinv_own = rown[...]
    mean = jnp.sum(dots, axis=1, keepdims=True) * (1.0 / D) * rinv_own
    ab[...] = rinv_own
    bb[...] = rinv_own * rinv_own * mean

    @pl.when(p == 3)
    def _():
        pltpu.make_async_copy(cin, cin, lsem.at[5]).wait()

    def c_copy(n):
        part = slab(n, T)
        return rcopy(cout.at[part], cin.at[part], src_.at[n], rrc.at[n], ((p + 3) % 4, i))

    for n in range(CHUNKS):
        @pl.when(p < 3)
        def _():
            c_copy(n).wait_recv()

        a = wide(ab[...], ROWS)
        b = wide(bb[...], ROWS)
        for m in range(T):
            branch = (sgr[slab(n), slab(m, ROWS)].astype(jnp.float32) * a
                      - xs[n * T + m].astype(jnp.float32) * b)
            cout[n * T + m] = (cin[n * T + m].astype(jnp.float32) + branch).astype(jnp.bfloat16)

        @pl.when(p > 0)
        def _():
            c_copy(n).start()

        for m in range(T):
            pltpu.make_async_copy(
                cout.at[n * T + m], o_in.at[0, :, x_cols(n * T + m)], osem.at[1]).start()

    for k in range(1, T):
        ws_copy(k).wait_recv()
        gs_copy(k).wait_recv()

    gtotal = gs[0:1, :]
    total = wown[...]
    for k in range(1, T):
        total = total + wrecv[slab(k, ROWS), :].astype(jnp.float32)
        gtotal = gtotal + grecv[k * 8:k * 8 + 1, :]
    wown[...] = total
    o_gain[...] = gtotal
    out_k = pltpu.make_async_copy(wown.at[:, 0:KVW], o_kw.at[0], osem.at[2])
    out_v = pltpu.make_async_copy(wown.at[:, KVW:], o_vw.at[0], osem.at[3])
    out_k.start()
    out_v.start()

    for k in range(1, F):
        x_copy(k).wait_send()
        r_copy(k).wait_send()
        p_copy(k).wait_send()
        ga_copy(k).wait_send()
        h_copy(k).wait_send()
    for k in range(1, T):
        w_copy(k).wait_send()
        g_copy(k).wait_send()
        ws_copy(k).wait_send()
        gs_copy(k).wait_send()
    for copy in (hop1, hop2, even1, even2, back_a, back_b, back_c, back_d):
        copy.wait_send()

    @pl.when(p > 0)
    def _():
        for n in range(CHUNKS):
            c_copy(n).wait_send()

    pltpu.make_async_copy(cout, cout, osem.at[1]).wait()
    for copy in (out_q, out_k, out_v):
        copy.wait()


def on_device(layer_input, queries, out_grad, top_grad, norm_gain, key_weight, value_weight,
              weight_exponents, doc_lengths):
    factors = jnp.exp2(weight_exponents.astype(jnp.float32)).reshape(16)
    half = np.arange(128) % 64
    freq = np.power(np.float64(THETA), -(half * 2.0 / HEAD)).astype(np.float32)
    freq = jnp.asarray(np.broadcast_to(freq, (8, 128)))
    bf, f32 = jnp.bfloat16, jnp.float32
    vmem = functools.partial(pltpu.VMEM)
    dma = pltpu.SemaphoreType.DMA
    hbm = pl.BlockSpec(memory_space=pl.ANY)
    smem = pl.BlockSpec(memory_space=pltpu.SMEM)
    vm = pl.BlockSpec(memory_space=pltpu.VMEM)
    scratch = [
        vmem((F * T, TOK, ROWS), bf),
        vmem((F * T, TOK, ROWS), bf),
        vmem((ROWS, KVW), bf),
        vmem((ROWS, KVW), bf),
        vmem((SLAB, SLAB), bf),
        vmem((8 * T, ROWS), f32),
        vmem((64, 128), f32),
        vmem((TOK, 128), f32),
        vmem((QW, HEAD), bf),
        vmem((QW, HEAD), bf),
        vmem((F * T, TOK, ROWS), bf),
        vmem((F * T, TOK, ROWS), bf),
        vmem((TOK, 128), f32),
        vmem((TOK, 128), f32),
        vmem((WIN, 128), f32),
        vmem((SLAB, SLAB), bf),
        vmem((SLAB, SLAB), bf),
        vmem((SLAB, SLAB), bf),
        vmem((SLAB, SLAB), bf),
        vmem((WIN, SLAB), bf),
        vmem((WIN, SLAB), bf),
        vmem((WIN, SLAB), bf),
        vmem((WIN, SLAB), bf),
        vmem((4 * TOK, SLAB), bf),
        vmem((TOK, QW), bf),
        vmem((SLAB, SLAB), bf),
        vmem((SLAB, SLAB), bf),
        vmem((SLAB, SLAB), bf),
        vmem((TOK, 128), f32),
        vmem((TOK, 128), f32),
        vmem((SLAB, SLAB), bf),
        vmem((SLAB, SLAB), bf),
        vmem((ROWS, SLAB), f32),
        vmem((8 * T, ROWS), f32),
        vmem((8 * T, ROWS), f32),
        vmem((8, SLAB), f32),
        dma((6,)), dma((F,)), dma((F,)), dma((F,)), dma((F,)),
        dma((T,)), dma((T,)), dma((T,)), dma((T,)), dma((F,)), dma((F,)),
        dma((4,)), dma((4,)), dma((4,)), dma((4,)),
        dma((F,)), dma((F,)), dma((F,)), dma((F,)),
        dma((T,)), dma((T,)), dma((T,)), dma((T,)),
        dma((CHUNKS,)), dma((CHUNKS,)), dma((4,)),
    ]
    o_in, o_q, o_kw, o_vw, o_gain = pl.pallas_call(
        kernel,
        out_shape=(
            jax.ShapeDtypeStruct((1, TOK, D), bf),
            jax.ShapeDtypeStruct((1, TOK, QW), bf),
            jax.ShapeDtypeStruct((1, ROWS, KVW), f32),
            jax.ShapeDtypeStruct((1, ROWS, KVW), f32),
            jax.ShapeDtypeStruct((1, ROWS), f32),
        ),
        in_specs=[smem, smem, vm, hbm, hbm, hbm, hbm, vm, hbm, hbm],
        out_specs=(hbm, hbm, hbm, hbm, vm),
        scratch_shapes=scratch,
        compiler_params=pltpu.CompilerParams(
            collective_id=0, has_side_effects=True, vmem_limit_bytes=60 * 1024 * 1024),
    )(factors, doc_lengths, freq, layer_input, queries, out_grad, top_grad, norm_gain,
      key_weight, value_weight)
    return o_in, o_q, o_kw, o_vw, o_gain


def solution(mesh):
    in_specs = (
        P("pipe", "dp", None),
        P("pipe", "dp", None),
        P("pipe", "dp", None),
        P("dp", None),
        P("pipe", "dp"),
        P("pipe", "dp", None),
        P("pipe", "dp", None),
        P("pipe", None, "dp", None),
        P(),
    )
    out_specs = (
        P("pipe", "dp", None),
        P("pipe", "dp", None),
        P("pipe", "dp", None),
        P("pipe", "dp", None),
        P("pipe", "dp"),
    )
    return jax.shard_map(
        on_device, mesh=mesh, in_specs=in_specs, out_specs=out_specs, check_vma=False
    )
```

```python
import functools
import math

import jax
import jax.numpy as jnp
import numpy as np
from jax import lax
from jax.experimental import pallas as pl
from jax.experimental.pallas import tpu as pltpu
from jax.sharding import PartitionSpec as P

D = 8192
KV_HEADS = 4
Q_PER_KV = 8
HEAD = 128
TOK = 128
REACH = 4
KVW = 512
QW = 4096
ROWS = 256
THETA = 500000.0
EPS = 1e-05
MASKED = -1e30

F = 8
T = 4
SLAB = 1024
WIN = (REACH + 1) * TOK
PAIR = 2

MESH = pl.DeviceIdType.MESH
NT = (((1,), (1,)), ((), ()))
NN = (((1,), (0,)), ((), ()))


def rows(start, size):
    return pl.ds(pl.multiple_of(start, size), size)


def cols(start, size):
    return pl.ds(pl.multiple_of(start, size), size)


def dot(a, b, dims=NN):
    return lax.dot_general(a, b, dims, preferred_element_type=jnp.float32)


def wide(col, width):
    return jnp.concatenate([col] * (width // col.shape[1]), axis=1)


def kernel(
    exps, docs, x, q, do, top, gain, kw, vw,
    o_in, o_q, o_kw, o_vw, o_gain,
    xs, xr, kwv, vwv, wr, gr, rr, rown, qs, dos, cin, cout, cosb, sinb, bias,
    hbuf, ht, proj, psend, precv, kwin, pt, dst, tb, ra, dq, gall, hgs, sgr, bb,
    ws, wrecv, wown, gs, grecv, gacc,
    lsem, sx, rx, sr, rrs, sw, rw, sg, rg, sp, rp, skv, rkv, sb, rb,
    sga, rga, sh, rh, sws, rws, sgs, rgs, src_, rrc, osem, lx,
):
    p = lax.axis_index("pipe")
    i = lax.axis_index("dp")
    f = i % F
    t = i // F
    xl = i % 2

    def slab(k, size=TOK):
        return slice(k * size, (k + 1) * size)

    def f_up(k):
        return (p, t * F + (f + k) % F)

    def f_down(k):
        return (p, t * F + (f + F - k) % F)

    def t_up(k):
        return (p, (t + k) % T * F + f)

    def t_down(k):
        return (p, (t + T - k) % T * F + f)

    def rcopy(src, dst, ssem, rsem, dev):
        return pltpu.make_async_remote_copy(
            src_ref=src, dst_ref=dst, send_sem=ssem, recv_sem=rsem,
            device_id=dev, device_id_type=MESH)

    def x_cols(n):
        return cols(((t + T - n % T) % T * F + (f + n // T) % F) * ROWS, ROWS)

    barrier = pltpu.get_barrier_semaphore()
    peers = [f_up(k) for k in range(1, F)] + [t_up(k) for k in range(1, T)]
    peers += [(p, (i + 2) % 32), (p, (i + 30) % 32)]
    peers += [((p + 1) % 4, i), ((p + 3) % 4, i)]
    for peer in peers:
        pl.semaphore_signal(barrier, inc=1, device_id=peer, device_id_type=MESH)

    def load_slab(k):
        def load(n, carry):
            pltpu.make_async_copy(
                x.at[0, :, x_cols(k * T + n)], xs.at[k * T + n], lx.at[k]).start()
            return carry

        lax.fori_loop(0, T, load, 0)

    order = list(range(1, F)) + [0]
    load_slab(order[0])
    pltpu.make_async_copy(kw.at[0], kwv, lsem.at[1]).start()
    pltpu.make_async_copy(vw.at[0], vwv, lsem.at[2]).start()
    for k in order[1:]:
        load_slab(k)
    pl.semaphore_wait(barrier, len(peers))

    def x_copy(k):
        return rcopy(xs.at[slab(k, T)], xr.at[slab(k, T)], sx.at[k], rx.at[k], f_up(k))

    def wait_slab(k):
        pltpu.make_async_copy(xs.at[slab(k, T)], xs.at[slab(k, T)], lx.at[k]).wait()

    early = 3
    for k in range(1, early):
        wait_slab(k)
        x_copy(k).start()

    pltpu.make_async_copy(kw.at[0], kwv, lsem.at[1]).wait()
    pltpu.make_async_copy(vw.at[0], vwv, lsem.at[2]).wait()
    for rblock in range(2):
        for cblock in range(4):
            for which, wv in ((0, kwv), (1, vwv)):
                block = wv[slab(rblock), slab(cblock)].astype(jnp.float32)
                power = exps[which * 8 + rblock * 4 + cblock]
                scaled = block * jnp.where(power > 0, 2.0, jnp.where(power < 0, 0.5, 1.0))
                wr[slab(rblock), slab(which * 4 + cblock)] = scaled.astype(jnp.bfloat16)
    gr[0:8, :] = jnp.broadcast_to(gain[...].astype(jnp.float32), (8, ROWS))

    def w_copy(k):
        return rcopy(wr.at[0:ROWS], wr.at[slab(k, ROWS)], sw.at[k], rw.at[k], t_up(k))

    def g_copy(k):
        return rcopy(gr.at[0:8], gr.at[slab(k, 8)], sg.at[k], rg.at[k], t_up(k))

    for k in range(1, T):
        g_copy(k).start()
        w_copy(k).start()

    for k in range(early, F):
        wait_slab(k)
    wait_slab(0)

    def add_squares(n, acc):
        part = xs[n].astype(jnp.float32)
        part = part * part
        for c in range(ROWS // 128):
            acc = acc + part[:, slab(c)]
        return acc

    squares = lax.fori_loop(0, F * T, add_squares, jnp.zeros((TOK, 128), jnp.float32))
    mean_sq = jnp.sum(squares, axis=1, keepdims=True) * (1.0 / D)
    rinv = jnp.broadcast_to(1.0 / jnp.sqrt(mean_sq + EPS), (TOK, 128))
    rown[...] = rinv
    rr[0:8, :] = rinv.T[0:8, :]

    def r_copy(k):
        return rcopy(rr.at[0:8], rr.at[slab(k, 8)], sr.at[k], rrs.at[k], f_up(k))

    for k in range(1, F):
        r_copy(k).start()
    for k in range(early, F):
        x_copy(k).start()
    xr[0:T] = xs[0:T]

    def load_q(n, carry):
        pltpu.make_async_copy(
            q.at[0, :, cols(n * HEAD, HEAD)], qs.at[rows(n * TOK, TOK)], lsem.at[3]).start()
        pltpu.make_async_copy(
            do.at[0, :, cols(n * HEAD, HEAD)], dos.at[rows(n * TOK, TOK)], lsem.at[4]).start()
        return carry

    lax.fori_loop(0, KV_HEADS * Q_PER_KV, load_q, 0)

    @pl.when(p == 3)
    def _():
        def load_top(n, carry):
            pltpu.make_async_copy(top.at[:, x_cols(n)], cin.at[n], lsem.at[5]).start()
            return carry

        lax.fori_loop(0, F * T, load_top, 0)

    tok_col = i * TOK + lax.broadcasted_iota(jnp.int32, (TOK, 128), 0)
    tok_row = i * TOK + lax.broadcasted_iota(jnp.int32, (8, 128), 1)

    def scan_docs(n, carry):
        start, scol, srow = carry
        scol = jnp.where(start <= tok_col, start, scol)
        srow = jnp.where(start <= tok_row, start, srow)
        return start + docs[n], scol, srow

    _, scol, srow = lax.fori_loop(
        0, 64, scan_docs,
        (jnp.int32(0), jnp.zeros((TOK, 128), jnp.int32), jnp.zeros((8, 128), jnp.int32)))
    lane = lax.broadcasted_iota(jnp.int32, (TOK, 128), 1)
    freq = jnp.ones((TOK, 128), jnp.float32)
    for bit in range(6):
        power = float(np.float64(THETA) ** (-(2.0 * 2 ** bit / HEAD)))
        freq = jnp.where((lane & (1 << bit)) != 0, freq * power, freq)
    angle = (tok_col - scol).astype(jnp.float32) * freq
    sine = jnp.sin(angle)
    cosb[...] = jnp.cos(angle)
    sinb[...] = jnp.where(lane < 64, -sine, sine)
    key_index = (i - REACH) * TOK + lax.broadcasted_iota(jnp.int32, (WIN, 128), 0)
    seen = (key_index >= srow[0:1, :]) & (key_index <= tok_row[0:1, :])
    bias[...] = jnp.where(seen, 0.0, MASKED)

    for k in range(1, T):
        w_copy(k).wait_recv()
        g_copy(k).wait_recv()

    def inv_rms(k):
        return jnp.broadcast_to(rr[k * 8:k * 8 + 1, :], (TOK, 128)).T

    def slab_x(k):
        return jnp.concatenate(
            [xr[k * T + n].astype(jnp.float32) for n in range(T)], axis=1)

    gain_row = jnp.concatenate([gr[n * 8:n * 8 + 1, :] for n in range(T)], axis=1)

    def p_copy(k):
        return rcopy(psend.at[slab(k)], precv.at[slab(k)], sp.at[k], rp.at[k], f_down(k))

    for k in range(F):
        if k > 0:
            x_copy(k).wait_recv()
            r_copy(k).wait_recv()
        hidden = (slab_x(k) * wide(inv_rms(k), SLAB) * gain_row).astype(jnp.bfloat16)
        hbuf[slab(k), :] = hidden
        part = dot(hidden, wr[...]).astype(jnp.bfloat16)
        if k > 0:
            psend[slab(k), :] = part
            p_copy(k).start()
        else:
            precv[slab(k), :] = part

    for k in range(F):
        ht[:, slab(k)] = hbuf[slab(k), :].T

    for k in range(1, F):
        p_copy(k).wait_recv()

    def rope(block, sign):
        return block * cosb[...] + pltpu.roll(block, 64, 1) * (sinb[...] * sign)

    for c in range(8):
        total = precv[0:TOK, slab(c)].astype(jnp.float32)
        for k in range(1, F):
            total = total + precv[slab(k), slab(c)].astype(jnp.float32)
        if c < 4:
            proj[:, slab(c)] = total
            total = rope(total, 1.0)
        else:
            proj[:, slab(c)] = total
        kwin[REACH * TOK:, slab(c)] = total.astype(jnp.bfloat16)

    partner = (p, i + 1 - 2 * xl)
    ahead = (p, (i + 2) % 32)
    back = (p, (i + 30) % 32)

    def kv_copy(src, dst_slot, n, dev):
        return rcopy(kwin.at[slab(src)], kwin.at[slab(dst_slot)], skv.at[n], rkv.at[n], dev)

    hop1 = kv_copy(4, 2, 0, ahead)
    hop2 = kv_copy(2, 0, 1, ahead)
    even1 = kv_copy(4, 3, 2, partner)
    even2 = kv_copy(2, 1, 3, partner)
    odd1 = kv_copy(2, 3, 2, partner)
    odd2 = kv_copy(0, 1, 3, partner)
    hop1.start()

    @pl.when(xl == 0)
    def _():
        even1.start()

    hop1.wait_recv()
    hop2.start()

    @pl.when(xl == 0)
    def _():
        even2.start()

    @pl.when(xl == 1)
    def _():
        odd1.start()

    hop2.wait_recv()

    @pl.when(xl == 1)
    def _():
        odd2.start()

    pltpu.make_async_copy(qs, qs, lsem.at[3]).wait()
    pltpu.make_async_copy(dos, dos, lsem.at[4]).wait()
    even1.wait_recv()
    even2.wait_recv()

    inv_root = 1.0 / math.sqrt(HEAD)

    def one_kv_head(h, carry):
        kcol = cols(h * HEAD, HEAD)
        vcol = cols(KVW + h * HEAD, HEAD)
        keys = kwin[:, kcol]
        vals = kwin[:, vcol]
        keys_t = keys.T

        def heads(g, carry2):
            width = PAIR * TOK
            qrow = rows((h * Q_PER_KV + g * PAIR) * TOK, width)
            scores = dot(keys, qs[qrow, :], NT) * inv_root + wide(bias[...], width)
            top_score = jnp.max(scores, axis=0, keepdims=True)
            expd = jnp.exp(scores - top_score)
            probs = expd * (1.0 / jnp.sum(expd, axis=0, keepdims=True))
            low = probs.astype(jnp.bfloat16)
            pgrad = dot(vals, dos[qrow, :], NT)
            delta = jnp.sum(low.astype(jnp.float32) * pgrad, axis=0, keepdims=True)
            sgrad = (probs * (pgrad - delta)).astype(jnp.bfloat16)
            pcol = cols(g * width, width)
            pt[:, pcol] = low
            dst[:, pcol] = sgrad
            dqt = dot(keys_t, sgrad) * inv_root
            for n in range(PAIR):
                head = (h * Q_PER_KV + g * PAIR + n) * HEAD
                dq[:, cols(head, HEAD)] = dqt[:, slab(n)].T.astype(jnp.bfloat16)
            return carry2

        lax.fori_loop(0, Q_PER_KV // PAIR, heads, 0)
        hrow = rows(h * Q_PER_KV * TOK, Q_PER_KV * TOK)
        tb[:, vcol] = dot(pt[...], dos[hrow, :]).astype(jnp.bfloat16)
        tb[:, kcol] = (dot(dst[...], qs[hrow, :]) * inv_root).astype(jnp.bfloat16)
        return carry

    lax.fori_loop(0, KV_HEADS, one_kv_head, 0)

    def t_copy(src, n, dev):
        return rcopy(tb.at[slab(src)], ra.at[slab(n)], sb.at[n], rb.at[n], dev)

    back_a = t_copy(3, 0, partner)
    back_b = t_copy(1, 1, partner)
    back_c = t_copy(0, 2, back)
    back_d = t_copy(2, 3, back)
    back_b.start()
    back_a.start()

    def fold(s, n):
        tb[slab(s), :] = (tb[slab(s), :].astype(jnp.float32)
                          + ra[slab(n), :].astype(jnp.float32)).astype(jnp.bfloat16)

    back_b.wait_recv()

    @pl.when(xl == 1)
    def _():
        fold(0, 1)

    back_c.start()
    back_a.wait_recv()

    @pl.when(xl == 1)
    def _():
        fold(2, 0)

    @pl.when(xl == 0)
    def _():
        fold(2, 1)
        fold(4, 0)

    back_c.wait_recv()
    fold(2, 2)
    back_d.start()
    out_q = pltpu.make_async_copy(dq, o_q.at[0], osem.at[0])
    out_q.start()
    back_d.wait_recv()
    dots = jnp.zeros((TOK, 128), jnp.float32)
    for c in range(8):
        total = (tb[slab(REACH), slab(c)].astype(jnp.float32)
                 + ra[slab(3), slab(c)].astype(jnp.float32))
        if c < 4:
            total = rope(total, -1.0)
        total = total.astype(jnp.bfloat16)
        gall[0:TOK, slab(c)] = total
        dots = dots + total.astype(jnp.float32) * proj[:, slab(c)]

    def ga_copy(k):
        return rcopy(gall.at[0:TOK], gall.at[slab(k)], sga.at[k], rga.at[k], f_up(k))

    for k in range(1, F):
        ga_copy(k).start()

    rinv_own = rown[...]
    mean = jnp.sum(dots, axis=1, keepdims=True) * (1.0 / D)
    bb[...] = rinv_own * rinv_own * mean

    gacc[...] = jnp.zeros_like(gacc)

    def h_copy(k):
        return rcopy(hgs.at[slab(k)], sgr.at[slab(k)], sh.at[k], rh.at[k], f_down(k))

    for k in range(F):
        if k > 0:
            ga_copy(k).wait_recv()
        hg = dot(gall[slab(k), :], wr[...], NT)
        scaled = (hg * gain_row).astype(jnp.bfloat16)
        if k > 0:
            hgs[slab(k), :] = scaled
            h_copy(k).start()
        else:
            sgr[slab(k), :] = scaled
        prod = hg * slab_x(k) * wide(inv_rms(k), SLAB)
        part = prod[0:8, :]
        for n in range(1, TOK // 8):
            part = part + prod[slab(n, 8), :]
        gacc[...] = gacc[...] + part

    gterm = jnp.broadcast_to(jnp.sum(gacc[...], axis=0, keepdims=True), (8, SLAB))
    for k in range(T):
        gs[slab(k, 8), :] = gterm[:, slab(k, ROWS)]

    def gs_copy(k):
        return rcopy(gs.at[slab(k, 8)], grecv.at[slab(k, 8)], sgs.at[k], rgs.at[k], t_down(k))

    def ws_copy(k):
        return rcopy(ws.at[slab(k, ROWS)], wrecv.at[slab(k, ROWS)], sws.at[k], rws.at[k],
                     t_down(k))

    def weight_term(k):
        if k == 0:
            wown[...] = dot(ht[0:ROWS, :], gall[...])
        else:
            ws[slab(k, ROWS), :] = dot(ht[slab(k, ROWS), :], gall[...]).astype(jnp.bfloat16)
            ws_copy(k).start()
            gs_copy(k).start()

    @pl.when(p == 3)
    def _():
        pltpu.make_async_copy(cin, cin, lsem.at[5]).wait()

    def c_copy(n):
        part = slab(n, T)
        return rcopy(cout.at[part], cin.at[part], src_.at[n], rrc.at[n], ((p + 3) % 4, i))

    for n in range(F):
        if n > 0:
            h_copy(n).wait_recv()

        @pl.when(p < 3)
        def _():
            c_copy(n).wait_recv()

        a = wide(rown[...], ROWS)
        b = wide(bb[...], ROWS)
        for m in range(T):
            branch = (sgr[slab(n), slab(m, ROWS)].astype(jnp.float32) * a
                      - xs[n * T + m].astype(jnp.float32) * b)
            cout[n * T + m] = (cin[n * T + m].astype(jnp.float32) + branch).astype(jnp.bfloat16)

        @pl.when(p > 0)
        def _():
            c_copy(n).start()

        for m in range(T):
            pltpu.make_async_copy(
                cout.at[n * T + m], o_in.at[0, :, x_cols(n * T + m)], osem.at[1]).start()
        if n < T:
            weight_term((n + 1) % T)

    for k in range(1, T):
        ws_copy(k).wait_recv()
        gs_copy(k).wait_recv()

    gtotal = gs[0:1, :]
    total = wown[...]
    for k in range(1, T):
        total = total + wrecv[slab(k, ROWS), :].astype(jnp.float32)
        gtotal = gtotal + grecv[k * 8:k * 8 + 1, :]
    wown[...] = total
    o_gain[...] = gtotal
    out_k = pltpu.make_async_copy(wown.at[:, 0:KVW], o_kw.at[0], osem.at[2])
    out_v = pltpu.make_async_copy(wown.at[:, KVW:], o_vw.at[0], osem.at[3])
    out_k.start()
    out_v.start()

    for k in range(1, F):
        x_copy(k).wait_send()
        r_copy(k).wait_send()
        p_copy(k).wait_send()
        ga_copy(k).wait_send()
        h_copy(k).wait_send()
    for k in range(1, T):
        w_copy(k).wait_send()
        g_copy(k).wait_send()
        ws_copy(k).wait_send()
        gs_copy(k).wait_send()
    for copy in (hop1, hop2, even1, even2, back_a, back_b, back_c, back_d):
        copy.wait_send()

    @pl.when(p > 0)
    def _():
        for n in range(F):
            c_copy(n).wait_send()

    pltpu.make_async_copy(cout, cout, osem.at[1]).wait()
    for copy in (out_q, out_k, out_v):
        copy.wait()


def on_device(layer_input, queries, out_grad, top_grad, norm_gain, key_weight, value_weight,
              weight_exponents, doc_lengths):
    bf, f32 = jnp.bfloat16, jnp.float32
    vmem = functools.partial(pltpu.VMEM)
    dma = pltpu.SemaphoreType.DMA
    hbm = pl.BlockSpec(memory_space=pl.ANY)
    smem = pl.BlockSpec(memory_space=pltpu.SMEM)
    vm = pl.BlockSpec(memory_space=pltpu.VMEM)
    scratch = [
        vmem((F * T, TOK, ROWS), bf),
        vmem((F * T, TOK, ROWS), bf),
        vmem((ROWS, KVW), bf),
        vmem((ROWS, KVW), bf),
        vmem((SLAB, SLAB), bf),
        vmem((8 * T, ROWS), f32),
        vmem((64, 128), f32),
        vmem((TOK, 128), f32),
        vmem((QW, HEAD), bf),
        vmem((QW, HEAD), bf),
        vmem((F * T, TOK, ROWS), bf),
        vmem((F * T, TOK, ROWS), bf),
        vmem((TOK, 128), f32),
        vmem((TOK, 128), f32),
        vmem((WIN, 128), f32),
        vmem((SLAB, SLAB), bf),
        vmem((SLAB, SLAB), bf),
        vmem((TOK, SLAB), f32),
        vmem((SLAB, SLAB), bf),
        vmem((SLAB, SLAB), bf),
        vmem((WIN, SLAB), bf),
        vmem((WIN, SLAB), bf),
        vmem((WIN, SLAB), bf),
        vmem((WIN, SLAB), bf),
        vmem((4 * TOK, SLAB), bf),
        vmem((TOK, QW), bf),
        vmem((SLAB, SLAB), bf),
        vmem((SLAB, SLAB), bf),
        vmem((SLAB, SLAB), bf),
        vmem((TOK, 128), f32),
        vmem((SLAB, SLAB), bf),
        vmem((SLAB, SLAB), bf),
        vmem((ROWS, SLAB), f32),
        vmem((8 * T, ROWS), f32),
        vmem((8 * T, ROWS), f32),
        vmem((8, SLAB), f32),
        dma((6,)), dma((F,)), dma((F,)), dma((F,)), dma((F,)),
        dma((T,)), dma((T,)), dma((T,)), dma((T,)), dma((F,)), dma((F,)),
        dma((4,)), dma((4,)), dma((4,)), dma((4,)),
        dma((F,)), dma((F,)), dma((F,)), dma((F,)),
        dma((T,)), dma((T,)), dma((T,)), dma((T,)),
        dma((F,)), dma((F,)), dma((4,)), dma((F,)),
    ]
    o_in, o_q, o_kw, o_vw, o_gain = pl.pallas_call(
        kernel,
        out_shape=(
            jax.ShapeDtypeStruct((1, TOK, D), bf),
            jax.ShapeDtypeStruct((1, TOK, QW), bf),
            jax.ShapeDtypeStruct((1, ROWS, KVW), f32),
            jax.ShapeDtypeStruct((1, ROWS, KVW), f32),
            jax.ShapeDtypeStruct((1, ROWS), f32),
        ),
        in_specs=[smem, smem, hbm, hbm, hbm, hbm, vm, hbm, hbm],
        out_specs=(hbm, hbm, hbm, hbm, vm),
        scratch_shapes=scratch,
        compiler_params=pltpu.CompilerParams(
            collective_id=0, has_side_effects=True, vmem_limit_bytes=60 * 1024 * 1024),
    )(weight_exponents.reshape(16), doc_lengths, layer_input, queries, out_grad, top_grad, norm_gain,
      key_weight, value_weight)
    return o_in, o_q, o_kw, o_vw, o_gain


def solution(mesh):
    in_specs = (
        P("pipe", "dp", None),
        P("pipe", "dp", None),
        P("pipe", "dp", None),
        P("dp", None),
        P("pipe", "dp"),
        P("pipe", "dp", None),
        P("pipe", "dp", None),
        P("pipe", None, "dp", None),
        P(),
    )
    out_specs = (
        P("pipe", "dp", None),
        P("pipe", "dp", None),
        P("pipe", "dp", None),
        P("pipe", "dp", None),
        P("pipe", "dp"),
    )
    return jax.shard_map(
        on_device, mesh=mesh, in_specs=in_specs, out_specs=out_specs, check_vma=False
    )
```

```python
import functools
import math

import jax
import jax.numpy as jnp
import numpy as np
from jax import lax
from jax.experimental import pallas as pl
from jax.experimental.pallas import tpu as pltpu
from jax.sharding import PartitionSpec as P

D = 8192
KV_HEADS = 4
Q_PER_KV = 8
HEAD = 128
TOK = 128
REACH = 4
KVW = 512
QW = 4096
ROWS = 256
THETA = 500000.0
EPS = 1e-05
MASKED = -1e30

F = 8
T = 4
SLAB = 1024
WIN = (REACH + 1) * TOK
PAIR = 2

MESH = pl.DeviceIdType.MESH
NT = (((1,), (1,)), ((), ()))
NN = (((1,), (0,)), ((), ()))


def rows(start, size):
    return pl.ds(pl.multiple_of(start, size), size)


def cols(start, size):
    return pl.ds(pl.multiple_of(start, size), size)


def dot(a, b, dims=NN):
    return lax.dot_general(a, b, dims, preferred_element_type=jnp.float32)


def wide(col, width):
    return jnp.concatenate([col] * (width // col.shape[1]), axis=1)


def kernel(
    exps, docs, x, q, do, top, gain, kw, vw,
    o_in, o_q, o_kw, o_vw, o_gain,
    xs, xr, kwv, vwv, wr, gr, rr, rown, qs, dos, cin, cout, cosb, sinb, bias,
    hbuf, ht, proj, psend, precv, kwin, pt, dst, tb, ra, dq, gall, hgs, sgr, bb,
    ws, wrecv, wown, gs, grecv, gacc,
    lsem, sx, rx, sr, rrs, sw, rw, sg, rg, sp, rp, skv, rkv, sb, rb,
    sga, rga, sh, rh, sws, rws, sgs, rgs, src_, rrc, osem, lx,
):
    p = lax.axis_index("pipe")
    i = lax.axis_index("dp")
    f = i % F
    t = i // F
    xl = i % 2

    def slab(k, size=TOK):
        return slice(k * size, (k + 1) * size)

    def f_up(k):
        return (p, t * F + (f + k) % F)

    def f_down(k):
        return (p, t * F + (f + F - k) % F)

    def t_up(k):
        return (p, (t + k) % T * F + f)

    def t_down(k):
        return (p, (t + T - k) % T * F + f)

    def rcopy(src, dst, ssem, rsem, dev):
        return pltpu.make_async_remote_copy(
            src_ref=src, dst_ref=dst, send_sem=ssem, recv_sem=rsem,
            device_id=dev, device_id_type=MESH)

    def x_cols(n):
        return cols(((t + T - n % T) % T * F + (f + n // T) % F) * ROWS, ROWS)

    barrier = pltpu.get_barrier_semaphore()
    peers = [f_up(k) for k in range(1, F)] + [t_up(k) for k in range(1, T)]
    peers += [(p, (i + 2) % 32), (p, (i + 30) % 32)]
    peers += [((p + 1) % 4, i), ((p + 3) % 4, i)]
    for peer in peers:
        pl.semaphore_signal(barrier, inc=1, device_id=peer, device_id_type=MESH)

    def load_slab(k):
        def load(n, carry):
            pltpu.make_async_copy(
                x.at[0, :, x_cols(k * T + n)], xs.at[k * T + n], lx.at[k]).start()
            return carry

        lax.fori_loop(0, T, load, 0)

    order = list(range(1, F)) + [0]
    load_slab(order[0])
    pltpu.make_async_copy(kw.at[0], kwv, lsem.at[1]).start()
    pltpu.make_async_copy(vw.at[0], vwv, lsem.at[2]).start()
    for k in order[1:]:
        load_slab(k)
    pl.semaphore_wait(barrier, len(peers))

    def x_copy(k):
        return rcopy(xs.at[slab(k, T)], xr.at[slab(k, T)], sx.at[k], rx.at[k], f_up(k))

    def wait_slab(k):
        pltpu.make_async_copy(xs.at[slab(k, T)], xs.at[slab(k, T)], lx.at[k]).wait()

    early = 3
    for k in range(1, early):
        wait_slab(k)
        x_copy(k).start()

    pltpu.make_async_copy(kw.at[0], kwv, lsem.at[1]).wait()
    pltpu.make_async_copy(vw.at[0], vwv, lsem.at[2]).wait()
    for rblock in range(2):
        for cblock in range(4):
            for which, wv in ((0, kwv), (1, vwv)):
                block = wv[slab(rblock), slab(cblock)].astype(jnp.float32)
                power = exps[0, which, rblock, cblock]
                place = cblock // 2 * 4 + which * 2 + cblock % 2
                scaled = block * jnp.where(power > 0, 2.0, jnp.where(power < 0, 0.5, 1.0))
                wr[slab(rblock), slab(place)] = scaled.astype(jnp.bfloat16)
    gr[0:8, :] = jnp.broadcast_to(gain[...].astype(jnp.float32), (8, ROWS))

    def w_copy(k):
        return rcopy(wr.at[0:ROWS], wr.at[slab(k, ROWS)], sw.at[k], rw.at[k], t_up(k))

    def g_copy(k):
        return rcopy(gr.at[0:8], gr.at[slab(k, 8)], sg.at[k], rg.at[k], t_up(k))

    for k in range(1, T):
        g_copy(k).start()
        w_copy(k).start()

    for k in range(early, F):
        wait_slab(k)
    wait_slab(0)

    def add_squares(n, acc):
        part = xs[n].astype(jnp.float32)
        part = part * part
        for c in range(ROWS // 128):
            acc = acc + part[:, slab(c)]
        return acc

    squares = lax.fori_loop(0, F * T, add_squares, jnp.zeros((TOK, 128), jnp.float32))
    mean_sq = jnp.sum(squares, axis=1, keepdims=True) * (1.0 / D)
    rinv = jnp.broadcast_to(1.0 / jnp.sqrt(mean_sq + EPS), (TOK, 128))
    rown[...] = rinv
    rr[0:8, :] = rinv.T[0:8, :]

    def r_copy(k):
        return rcopy(rr.at[0:8], rr.at[slab(k, 8)], sr.at[k], rrs.at[k], f_up(k))

    for k in range(1, F):
        r_copy(k).start()
    for k in range(early, F):
        x_copy(k).start()
    xr[0:T] = xs[0:T]

    def load_q(n, carry):
        pltpu.make_async_copy(
            q.at[0, :, cols(n * HEAD, HEAD)], qs.at[rows(n * TOK, TOK)], lsem.at[3]).start()
        pltpu.make_async_copy(
            do.at[0, :, cols(n * HEAD, HEAD)], dos.at[rows(n * TOK, TOK)], lsem.at[4]).start()
        return carry

    lax.fori_loop(0, KV_HEADS * Q_PER_KV, load_q, 0)

    @pl.when(p == 3)
    def _():
        def load_top(n, carry):
            pltpu.make_async_copy(top.at[:, x_cols(n)], cin.at[n], lsem.at[5]).start()
            return carry

        lax.fori_loop(0, F * T, load_top, 0)

    tok_col = i * TOK + lax.broadcasted_iota(jnp.int32, (TOK, 128), 0)
    tok_row = i * TOK + lax.broadcasted_iota(jnp.int32, (8, 128), 1)

    def scan_docs(n, carry):
        start, scol, srow = carry
        scol = jnp.where(start <= tok_col, start, scol)
        srow = jnp.where(start <= tok_row, start, srow)
        return start + docs[n], scol, srow

    _, scol, srow = lax.fori_loop(
        0, 64, scan_docs,
        (jnp.int32(0), jnp.zeros((TOK, 128), jnp.int32), jnp.zeros((8, 128), jnp.int32)))
    lane = lax.broadcasted_iota(jnp.int32, (TOK, 128), 1)
    freq = jnp.ones((TOK, 128), jnp.float32)
    for bit in range(6):
        power = float(np.float64(THETA) ** (-(2.0 * 2 ** bit / HEAD)))
        freq = jnp.where((lane & (1 << bit)) != 0, freq * power, freq)
    angle = (tok_col - scol).astype(jnp.float32) * freq
    sine = jnp.sin(angle)
    cosb[...] = jnp.cos(angle)
    sinb[...] = jnp.where(lane < 64, -sine, sine)
    key_index = (i - REACH) * TOK + lax.broadcasted_iota(jnp.int32, (WIN, 128), 0)
    seen = (key_index >= srow[0:1, :]) & (key_index <= tok_row[0:1, :])
    bias[...] = jnp.where(seen, 0.0, MASKED)

    for k in range(1, T):
        w_copy(k).wait_recv()
        g_copy(k).wait_recv()

    def inv_rms(k):
        return jnp.broadcast_to(rr[k * 8:k * 8 + 1, :], (TOK, 128)).T

    def slab_x(k):
        return jnp.concatenate(
            [xr[k * T + n].astype(jnp.float32) for n in range(T)], axis=1)

    gain_row = jnp.concatenate([gr[n * 8:n * 8 + 1, :] for n in range(T)], axis=1)

    def half_slab(u, k):
        return slab(u * F + k)

    def p_copy(u, k):
        return rcopy(psend.at[half_slab(u, k)], precv.at[half_slab(u, k)],
                     sp.at[u * F + k], rp.at[u * F + k], f_down(k))

    for k in range(F):
        if k > 0:
            x_copy(k).wait_recv()
            r_copy(k).wait_recv()
        hidden = (slab_x(k) * wide(inv_rms(k), SLAB) * gain_row).astype(jnp.bfloat16)
        hbuf[slab(k), :] = hidden
        part = dot(hidden, wr[...]).astype(jnp.bfloat16)
        for u in range(2):
            target = psend if k > 0 else precv
            target[half_slab(u, k), :] = part[:, slab(u, KVW)]
        if k > 0:
            p_copy(0, k).start()
    for k in range(1, F):
        p_copy(1, k).start()

    for k in range(F):
        ht[:, slab(k)] = hbuf[slab(k), :].T

    def rope(block, sign):
        return block * cosb[...] + pltpu.roll(block, 64, 1) * (sinb[...] * sign)

    partner = (p, i + 1 - 2 * xl)
    ahead = (p, (i + 2) % 32)
    back = (p, (i + 30) % 32)

    def slot(u, s):
        return slab(u * (REACH + 1) + s)

    def own_block(u):
        for k in range(1, F):
            p_copy(u, k).wait_recv()
        for c in range(4):
            total = precv[half_slab(u, 0), slab(c)].astype(jnp.float32)
            for k in range(1, F):
                total = total + precv[half_slab(u, k), slab(c)].astype(jnp.float32)
            proj[:, slab(u * 4 + c)] = total
            if c < 2:
                total = rope(total, 1.0)
            kwin[slot(u, REACH), slab(c)] = total.astype(jnp.bfloat16)

    class Window:
        def __init__(self, u):
            def copy(src, dst_slot, n, dev):
                return rcopy(kwin.at[slot(u, src)], kwin.at[slot(u, dst_slot)],
                             skv.at[u * 4 + n], rkv.at[u * 4 + n], dev)

            self.hop1 = copy(4, 2, 0, ahead)
            self.hop2 = copy(2, 0, 1, ahead)
            self.even1 = copy(4, 3, 2, partner)
            self.even2 = copy(2, 1, 3, partner)
            self.odd1 = copy(2, 3, 2, partner)
            self.odd2 = copy(0, 1, 3, partner)

        def first(self):
            self.hop1.start()

            @pl.when(xl == 0)
            def _():
                self.even1.start()

        def second(self):
            self.hop1.wait_recv()
            self.hop2.start()

            @pl.when(xl == 0)
            def _():
                self.even2.start()

            @pl.when(xl == 1)
            def _():
                self.odd1.start()

        def third(self):
            self.hop2.wait_recv()

            @pl.when(xl == 1)
            def _():
                self.odd2.start()

        def last(self):
            self.even1.wait_recv()
            self.even2.wait_recv()

        def sent(self):
            for copy in (self.hop1, self.hop2, self.even1, self.even2):
                copy.wait_send()

    inv_root = 1.0 / math.sqrt(HEAD)
    steps = Q_PER_KV // PAIR

    def attend(h, first, last):
        u, c = h // 2, h % 2
        window = slice(u * WIN, (u + 1) * WIN)
        keys = kwin[window, slab(c)]
        vals = kwin[window, slab(2 + c)]
        keys_t = keys.T

        def heads(g, carry):
            width = PAIR * TOK
            qrow = rows((h * Q_PER_KV + g * PAIR) * TOK, width)
            scores = dot(keys, qs[qrow, :], NT) * inv_root + wide(bias[...], width)
            top_score = jnp.max(scores, axis=0, keepdims=True)
            expd = jnp.exp(scores - top_score)
            probs = expd * (1.0 / jnp.sum(expd, axis=0, keepdims=True))
            low = probs.astype(jnp.bfloat16)
            pgrad = dot(vals, dos[qrow, :], NT)
            delta = jnp.sum(low.astype(jnp.float32) * pgrad, axis=0, keepdims=True)
            sgrad = (probs * (pgrad - delta)).astype(jnp.bfloat16)
            pcol = cols(g * width, width)
            pt[:, pcol] = low
            dst[:, pcol] = sgrad
            dqt = dot(keys_t, sgrad) * inv_root
            for n in range(PAIR):
                head = (h * Q_PER_KV + g * PAIR + n) * HEAD
                dq[:, cols(head, HEAD)] = dqt[:, slab(n)].T.astype(jnp.bfloat16)
            return carry

        lax.fori_loop(first, last, heads, 0)
        if last == steps:
            hrow = slab(h, Q_PER_KV * TOK)
            tb[window, slab(2 + c)] = dot(pt[...], dos[hrow, :]).astype(jnp.bfloat16)
            tb[window, slab(c)] = (dot(dst[...], qs[hrow, :]) * inv_root).astype(jnp.bfloat16)

    class Terms:
        def __init__(self, u):
            def copy(src, n, dev):
                return rcopy(tb.at[slot(u, src)], ra.at[slab(u * 4 + n)],
                             sb.at[u * 4 + n], rb.at[u * 4 + n], dev)

            self.u = u
            self.a = copy(3, 0, partner)
            self.b = copy(1, 1, partner)
            self.c = copy(0, 2, back)
            self.d = copy(2, 3, back)

        def fold(self, s, n):
            at = slot(self.u, s)
            tb[at, :] = (tb[at, :].astype(jnp.float32)
                         + ra[slab(self.u * 4 + n), :].astype(jnp.float32)).astype(jnp.bfloat16)

        def first(self):
            @pl.when(xl == 0)
            def _():
                self.c.start()

            self.b.start()
            self.a.start()

        def second(self):
            self.b.wait_recv()

            @pl.when(xl == 1)
            def _():
                self.fold(0, 1)
                self.c.start()

            self.a.wait_recv()

            @pl.when(xl == 1)
            def _():
                self.fold(2, 0)

            @pl.when(xl == 0)
            def _():
                self.fold(2, 1)
                self.fold(4, 0)

        def third(self):
            self.c.wait_recv()
            self.fold(2, 2)
            self.d.start()

        def last(self):
            u = self.u
            self.d.wait_recv()
            for c in range(4):
                total = (tb[slot(u, REACH), slab(c)].astype(jnp.float32)
                         + ra[slab(u * 4 + 3), slab(c)].astype(jnp.float32))
                if c < 2:
                    total = rope(total, -1.0)
                gall[half_slab(u, 0), slab(c)] = total.astype(jnp.bfloat16)
            for k in range(1, F):
                ga_copy(u, k).start()

        def sent(self):
            for copy in (self.a, self.b, self.c, self.d):
                copy.wait_send()

    def ga_copy(u, k):
        return rcopy(gall.at[half_slab(u, 0)], gall.at[half_slab(u, k)],
                     sga.at[u * F + k], rga.at[u * F + k], f_up(k))

    windows = [Window(0), Window(1)]
    terms = [Terms(0), Terms(1)]
    own_block(0)
    windows[0].first()
    pltpu.make_async_copy(qs, qs, lsem.at[3]).wait()
    pltpu.make_async_copy(dos, dos, lsem.at[4]).wait()
    windows[0].second()
    windows[0].third()
    own_block(1)
    windows[1].first()
    windows[0].last()
    attend(0, 0, steps // 2)
    windows[1].second()
    attend(0, steps // 2, steps)
    attend(1, 0, steps // 2)
    windows[1].third()
    attend(1, steps // 2, steps)
    terms[0].first()
    windows[1].last()
    attend(2, 0, steps)
    terms[0].second()
    attend(3, 0, steps // 2)
    terms[0].third()
    attend(3, steps // 2, steps)
    terms[1].first()
    out_q = pltpu.make_async_copy(dq, o_q.at[0], osem.at[0])
    out_q.start()
    terms[0].last()
    terms[1].second()
    terms[1].third()
    terms[1].last()

    dots = jnp.zeros((TOK, 128), jnp.float32)
    for u in range(2):
        for c in range(4):
            dots = dots + (gall[half_slab(u, 0), slab(c)].astype(jnp.float32)
                           * proj[:, slab(u * 4 + c)])
    rinv_own = rown[...]
    mean = jnp.sum(dots, axis=1, keepdims=True) * (1.0 / D)
    bb[...] = rinv_own * rinv_own * mean

    gacc[...] = jnp.zeros_like(gacc)

    def h_copy(k):
        return rcopy(hgs.at[slab(k)], sgr.at[slab(k)], sh.at[k], rh.at[k], f_down(k))

    for k in range(F):
        if k > 0:
            ga_copy(0, k).wait_recv()
            ga_copy(1, k).wait_recv()
        hg = (dot(gall[half_slab(0, k), :], wr[:, 0:KVW], NT)
              + dot(gall[half_slab(1, k), :], wr[:, KVW:], NT))
        scaled = (hg * gain_row).astype(jnp.bfloat16)
        if k > 0:
            hgs[slab(k), :] = scaled
            h_copy(k).start()
        else:
            sgr[slab(k), :] = scaled
        prod = hg * slab_x(k) * wide(inv_rms(k), SLAB)
        part = prod[0:8, :]
        for n in range(1, TOK // 8):
            part = part + prod[slab(n, 8), :]
        gacc[...] = gacc[...] + part

    gterm = jnp.broadcast_to(jnp.sum(gacc[...], axis=0, keepdims=True), (8, SLAB))
    for k in range(T):
        gs[slab(k, 8), :] = gterm[:, slab(k, ROWS)]

    def gs_copy(k):
        return rcopy(gs.at[slab(k, 8)], grecv.at[slab(k, 8)], sgs.at[k], rgs.at[k], t_down(k))

    def ws_copy(k):
        return rcopy(ws.at[slab(k, ROWS)], wrecv.at[slab(k, ROWS)], sws.at[k], rws.at[k],
                     t_down(k))

    def weight_term(k):
        for u in range(2):
            term = dot(ht[slab(k, ROWS), :], gall[slab(u, SLAB), :])
            if k == 0:
                wown[:, slab(u, KVW)] = term
            else:
                ws[slab(k, ROWS), slab(u, KVW)] = term.astype(jnp.bfloat16)
        if k > 0:
            ws_copy(k).start()
            gs_copy(k).start()

    @pl.when(p == 3)
    def _():
        pltpu.make_async_copy(cin, cin, lsem.at[5]).wait()

    def c_copy(n):
        part = slab(n, T)
        return rcopy(cout.at[part], cin.at[part], src_.at[n], rrc.at[n], ((p + 3) % 4, i))

    for n in range(F):
        if n > 0:
            h_copy(n).wait_recv()

        @pl.when(p < 3)
        def _():
            c_copy(n).wait_recv()

        a = wide(rown[...], ROWS)
        b = wide(bb[...], ROWS)
        for m in range(T):
            branch = (sgr[slab(n), slab(m, ROWS)].astype(jnp.float32) * a
                      - xs[n * T + m].astype(jnp.float32) * b)
            cout[n * T + m] = (cin[n * T + m].astype(jnp.float32) + branch).astype(jnp.bfloat16)

        @pl.when(p > 0)
        def _():
            c_copy(n).start()

        for m in range(T):
            pltpu.make_async_copy(
                cout.at[n * T + m], o_in.at[0, :, x_cols(n * T + m)], osem.at[1]).start()
        if n < T:
            weight_term((n + 1) % T)

    for k in range(1, T):
        ws_copy(k).wait_recv()
        gs_copy(k).wait_recv()

    gtotal = gs[0:1, :]
    total = wown[...]
    for k in range(1, T):
        total = total + wrecv[slab(k, ROWS), :].astype(jnp.float32)
        gtotal = gtotal + grecv[k * 8:k * 8 + 1, :]
    wown[...] = total
    o_gain[...] = gtotal
    outs = []
    for u in range(2):
        for which, out in ((0, o_kw), (1, o_vw)):
            outs.append(pltpu.make_async_copy(
                wown.at[:, slab(u * 2 + which, 256)], out.at[0, :, slab(u, 256)],
                osem.at[2 + u * 2 + which]))
            outs[-1].start()

    for k in range(1, F):
        x_copy(k).wait_send()
        r_copy(k).wait_send()
        for u in range(2):
            p_copy(u, k).wait_send()
            ga_copy(u, k).wait_send()
        h_copy(k).wait_send()
    for k in range(1, T):
        w_copy(k).wait_send()
        g_copy(k).wait_send()
        ws_copy(k).wait_send()
        gs_copy(k).wait_send()
    for member in windows + terms:
        member.sent()

    @pl.when(p > 0)
    def _():
        for n in range(F):
            c_copy(n).wait_send()

    pltpu.make_async_copy(cout, cout, osem.at[1]).wait()
    for copy in [out_q] + outs:
        copy.wait()


def on_device(layer_input, queries, out_grad, top_grad, norm_gain, key_weight, value_weight,
              weight_exponents, doc_lengths):
    bf, f32 = jnp.bfloat16, jnp.float32
    vmem = functools.partial(pltpu.VMEM)
    dma = pltpu.SemaphoreType.DMA
    hbm = pl.BlockSpec(memory_space=pl.ANY)
    smem = pl.BlockSpec(memory_space=pltpu.SMEM)
    vm = pl.BlockSpec(memory_space=pltpu.VMEM)
    scratch = [
        vmem((F * T, TOK, ROWS), bf),
        vmem((F * T, TOK, ROWS), bf),
        vmem((ROWS, KVW), bf),
        vmem((ROWS, KVW), bf),
        vmem((SLAB, SLAB), bf),
        vmem((8 * T, ROWS), f32),
        vmem((64, 128), f32),
        vmem((TOK, 128), f32),
        vmem((QW, HEAD), bf),
        vmem((QW, HEAD), bf),
        vmem((F * T, TOK, ROWS), bf),
        vmem((F * T, TOK, ROWS), bf),
        vmem((TOK, 128), f32),
        vmem((TOK, 128), f32),
        vmem((WIN, 128), f32),
        vmem((SLAB, SLAB), bf),
        vmem((SLAB, SLAB), bf),
        vmem((TOK, SLAB), f32),
        vmem((2 * SLAB, KVW), bf),
        vmem((2 * SLAB, KVW), bf),
        vmem((2 * WIN, KVW), bf),
        vmem((WIN, SLAB), bf),
        vmem((WIN, SLAB), bf),
        vmem((2 * WIN, KVW), bf),
        vmem((8 * TOK, KVW), bf),
        vmem((TOK, QW), bf),
        vmem((2 * SLAB, KVW), bf),
        vmem((SLAB, SLAB), bf),
        vmem((SLAB, SLAB), bf),
        vmem((TOK, 128), f32),
        vmem((SLAB, SLAB), bf),
        vmem((SLAB, SLAB), bf),
        vmem((ROWS, SLAB), f32),
        vmem((8 * T, ROWS), f32),
        vmem((8 * T, ROWS), f32),
        vmem((8, SLAB), f32),
        dma((6,)), dma((F,)), dma((F,)), dma((F,)), dma((F,)),
        dma((T,)), dma((T,)), dma((T,)), dma((T,)), dma((2 * F,)), dma((2 * F,)),
        dma((8,)), dma((8,)), dma((8,)), dma((8,)),
        dma((2 * F,)), dma((2 * F,)), dma((F,)), dma((F,)),
        dma((T,)), dma((T,)), dma((T,)), dma((T,)),
        dma((F,)), dma((F,)), dma((6,)), dma((F,)),
    ]
    o_in, o_q, o_kw, o_vw, o_gain = pl.pallas_call(
        kernel,
        out_shape=(
            jax.ShapeDtypeStruct((1, TOK, D), bf),
            jax.ShapeDtypeStruct((1, TOK, QW), bf),
            jax.ShapeDtypeStruct((1, ROWS, KVW), f32),
            jax.ShapeDtypeStruct((1, ROWS, KVW), f32),
            jax.ShapeDtypeStruct((1, ROWS), f32),
        ),
        in_specs=[smem, smem, hbm, hbm, hbm, hbm, vm, hbm, hbm],
        out_specs=(hbm, hbm, hbm, hbm, vm),
        scratch_shapes=scratch,
        compiler_params=pltpu.CompilerParams(
            collective_id=0, has_side_effects=True, vmem_limit_bytes=60 * 1024 * 1024),
    )(weight_exponents, doc_lengths, layer_input, queries, out_grad, top_grad, norm_gain,
      key_weight, value_weight)
    return o_in, o_q, o_kw, o_vw, o_gain


def solution(mesh):
    in_specs = (
        P("pipe", "dp", None),
        P("pipe", "dp", None),
        P("pipe", "dp", None),
        P("dp", None),
        P("pipe", "dp"),
        P("pipe", "dp", None),
        P("pipe", "dp", None),
        P("pipe", None, "dp", None),
        P(),
    )
    out_specs = (
        P("pipe", "dp", None),
        P("pipe", "dp", None),
        P("pipe", "dp", None),
        P("pipe", "dp", None),
        P("pipe", "dp"),
    )
    return jax.shard_map(
        on_device, mesh=mesh, in_specs=in_specs, out_specs=out_specs, check_vma=False
    )
```

```python
import functools
import math

import jax
import jax.numpy as jnp
import numpy as np
from jax import lax
from jax.experimental import pallas as pl
from jax.experimental.pallas import tpu as pltpu
from jax.sharding import PartitionSpec as P

D = 8192
KV_HEADS = 4
Q_PER_KV = 8
HEAD = 128
TOK = 128
REACH = 4
KVW = 512
QW = 4096
ROWS = 256
THETA = 500000.0
EPS = 1e-05
MASKED = -1e30

F = 8
T = 4
SLAB = 1024
WIN = (REACH + 1) * TOK
PAIR = 2
ORDER = (0, 2, 6, 4, 3, 5, 1, 7)

MESH = pl.DeviceIdType.MESH
NT = (((1,), (1,)), ((), ()))
NN = (((1,), (0,)), ((), ()))


def rows(start, size):
    return pl.ds(pl.multiple_of(start, size), size)


def cols(start, size):
    return pl.ds(pl.multiple_of(start, size), size)


def dot(a, b, dims=NN):
    return lax.dot_general(a, b, dims, preferred_element_type=jnp.float32)


def wide(col, width):
    return jnp.concatenate([col] * (width // col.shape[1]), axis=1)


def kernel(
    exps, docs, x, q, do, top, gain, kw, vw,
    o_in, o_q, o_kw, o_vw, o_gain,
    xs, xr, kwv, vwv, wr, gr, rr, rown, qs, dos, cin, cout, cosb, sinb, bias,
    hbuf, ht, proj, psend, precv, kwin, pt, dst, tb, ra, dq, gall, hgs, sgr, bb,
    ws, wrecv, wown, gs, grecv, gacc,
    lsem, sx, rx, sr, rrs, sw, rw, sg, rg, sp, rp, skv, rkv, sb, rb,
    sga, rga, sh, rh, sws, rws, sgs, rgs, src_, rrc, osem, lx,
):
    p = lax.axis_index("pipe")
    i = lax.axis_index("dp")
    f = i % F
    t = i // F
    xl = i % 2

    def slab(k, size=TOK):
        return slice(k * size, (k + 1) * size)

    def f_up(k):
        return (p, t * F + (f + k) % F)

    def f_down(k):
        return (p, t * F + (f + F - k) % F)

    def t_up(k):
        return (p, (t + k) % T * F + f)

    def t_down(k):
        return (p, (t + T - k) % T * F + f)

    def rcopy(src, dst, ssem, rsem, dev):
        return pltpu.make_async_remote_copy(
            src_ref=src, dst_ref=dst, send_sem=ssem, recv_sem=rsem,
            device_id=dev, device_id_type=MESH)

    def x_cols(n):
        return cols(((t + T - n % T) % T * F + (f + n // T) % F) * ROWS, ROWS)

    barrier = pltpu.get_barrier_semaphore()
    peers = [f_up(k) for k in range(1, F)] + [t_up(k) for k in range(1, T)]
    peers += [(p, (i + 2) % 32), (p, (i + 30) % 32)]
    peers += [((p + 1) % 4, i), ((p + 3) % 4, i)]
    for peer in peers:
        pl.semaphore_signal(barrier, inc=1, device_id=peer, device_id_type=MESH)

    def load_slab(k):
        def load(n, carry):
            pltpu.make_async_copy(
                x.at[0, :, x_cols(k * T + n)], xs.at[k * T + n], lx.at[k]).start()
            return carry

        lax.fori_loop(0, T, load, 0)

    order = list(range(1, F)) + [0]
    load_slab(order[0])
    pltpu.make_async_copy(kw.at[0], kwv, lsem.at[1]).start()
    pltpu.make_async_copy(vw.at[0], vwv, lsem.at[2]).start()
    for k in order[1:]:
        load_slab(k)
    pl.semaphore_wait(barrier, len(peers))

    def x_copy(k):
        return rcopy(xs.at[slab(k, T)], xr.at[slab(k, T)], sx.at[k], rx.at[k], f_up(k))

    def wait_slab(k):
        pltpu.make_async_copy(xs.at[slab(k, T)], xs.at[slab(k, T)], lx.at[k]).wait()

    early = 3
    for k in range(1, early):
        wait_slab(k)
        x_copy(k).start()

    pltpu.make_async_copy(kw.at[0], kwv, lsem.at[1]).wait()
    pltpu.make_async_copy(vw.at[0], vwv, lsem.at[2]).wait()
    for rblock in range(2):
        for cblock in range(4):
            for which, wv in ((0, kwv), (1, vwv)):
                block = wv[slab(rblock), slab(cblock)].astype(jnp.float32)
                power = exps[0, which, rblock, cblock]
                place = cblock // 2 * 4 + which * 2 + cblock % 2
                scaled = block * jnp.where(power > 0, 2.0, jnp.where(power < 0, 0.5, 1.0))
                wr[slab(rblock), slab(place)] = scaled.astype(jnp.bfloat16)
    gr[0:8, :] = jnp.broadcast_to(gain[...].astype(jnp.float32), (8, ROWS))

    def w_copy(k):
        return rcopy(wr.at[0:ROWS], wr.at[slab(k, ROWS)], sw.at[k], rw.at[k], t_up(k))

    def g_copy(k):
        return rcopy(gr.at[0:8], gr.at[slab(k, 8)], sg.at[k], rg.at[k], t_up(k))

    for k in range(1, T):
        g_copy(k).start()
        w_copy(k).start()

    for k in range(early, F):
        wait_slab(k)
    wait_slab(0)

    def add_squares(n, acc):
        part = xs[n].astype(jnp.float32)
        part = part * part
        for c in range(ROWS // 128):
            acc = acc + part[:, slab(c)]
        return acc

    squares = lax.fori_loop(0, F * T, add_squares, jnp.zeros((TOK, 128), jnp.float32))
    mean_sq = jnp.sum(squares, axis=1, keepdims=True) * (1.0 / D)
    rinv = jnp.broadcast_to(1.0 / jnp.sqrt(mean_sq + EPS), (TOK, 128))
    rown[...] = rinv
    rr[0:8, :] = rinv.T[0:8, :]

    def r_copy(k):
        return rcopy(rr.at[0:8], rr.at[slab(k, 8)], sr.at[k], rrs.at[k], f_up(k))

    for k in range(1, F):
        r_copy(k).start()
    for k in range(early, F):
        x_copy(k).start()
    xr[0:T] = xs[0:T]

    def load_q(n, carry):
        pltpu.make_async_copy(
            q.at[0, :, cols(n * HEAD, HEAD)], qs.at[rows(n * TOK, TOK)], lsem.at[3]).start()
        pltpu.make_async_copy(
            do.at[0, :, cols(n * HEAD, HEAD)], dos.at[rows(n * TOK, TOK)], lsem.at[4]).start()
        return carry

    lax.fori_loop(0, KV_HEADS * Q_PER_KV, load_q, 0)

    @pl.when(p == 3)
    def _():
        def load_top(n, carry):
            pltpu.make_async_copy(top.at[:, x_cols(n)], cin.at[n], lsem.at[5]).start()
            return carry

        lax.fori_loop(0, F * T, load_top, 0)

    tok_col = i * TOK + lax.broadcasted_iota(jnp.int32, (TOK, 128), 0)
    tok_row = i * TOK + lax.broadcasted_iota(jnp.int32, (8, 128), 1)

    def scan_docs(n, carry):
        start, scol, srow = carry
        scol = jnp.where(start <= tok_col, start, scol)
        srow = jnp.where(start <= tok_row, start, srow)
        return start + docs[n], scol, srow

    _, scol, srow = lax.fori_loop(
        0, 64, scan_docs,
        (jnp.int32(0), jnp.zeros((TOK, 128), jnp.int32), jnp.zeros((8, 128), jnp.int32)))
    lane = lax.broadcasted_iota(jnp.int32, (TOK, 128), 1)
    freq = jnp.ones((TOK, 128), jnp.float32)
    for bit in range(6):
        power = float(np.float64(THETA) ** (-(2.0 * 2 ** bit / HEAD)))
        freq = jnp.where((lane & (1 << bit)) != 0, freq * power, freq)
    angle = (tok_col - scol).astype(jnp.float32) * freq
    sine = jnp.sin(angle)
    cosb[...] = jnp.cos(angle)
    sinb[...] = jnp.where(lane < 64, -sine, sine)
    key_index = (i - REACH) * TOK + lax.broadcasted_iota(jnp.int32, (WIN, 128), 0)
    seen = (key_index >= srow[0:1, :]) & (key_index <= tok_row[0:1, :])
    bias[...] = jnp.where(seen, 0.0, MASKED)

    for k in range(1, T):
        w_copy(k).wait_recv()
        g_copy(k).wait_recv()

    def inv_rms(k):
        return jnp.broadcast_to(rr[k * 8:k * 8 + 1, :], (TOK, 128)).T

    def slab_x(k):
        return jnp.concatenate(
            [xr[k * T + n].astype(jnp.float32) for n in range(T)], axis=1)

    gain_row = jnp.concatenate([gr[n * 8:n * 8 + 1, :] for n in range(T)], axis=1)

    def half_slab(u, k):
        return slab(u * F + k)

    def p_copy(u, k):
        return rcopy(psend.at[half_slab(u, k)], precv.at[half_slab(u, k)],
                     sp.at[u * F + k], rp.at[u * F + k], f_down(k))

    for k in range(F):
        if k > 0:
            x_copy(k).wait_recv()
            r_copy(k).wait_recv()
        hidden = (slab_x(k) * wide(inv_rms(k), SLAB) * gain_row).astype(jnp.bfloat16)
        hbuf[slab(k), :] = hidden
        part = dot(hidden, wr[...]).astype(jnp.bfloat16)
        for u in range(2):
            target = psend if k > 0 else precv
            target[half_slab(u, k), :] = part[:, slab(u, KVW)]
        if k > 0:
            p_copy(0, k).start()
    for k in range(1, F):
        p_copy(1, k).start()

    for k in range(F):
        ht[:, slab(k)] = hbuf[slab(k), :].T

    def rope(block, sign):
        return block * cosb[...] + pltpu.roll(block, 64, 1) * (sinb[...] * sign)

    partner = (p, i + 1 - 2 * xl)
    ahead = (p, (i + 2) % 32)
    back = (p, (i + 30) % 32)

    def slot(u, s):
        return slab(u * (REACH + 1) + s)

    def own_block(u):
        for k in range(1, F):
            p_copy(u, k).wait_recv()
        for c in range(4):
            total = precv[half_slab(u, 0), slab(c)].astype(jnp.float32)
            for k in range(1, F):
                total = total + precv[half_slab(u, k), slab(c)].astype(jnp.float32)
            proj[:, slab(u * 4 + c)] = total
            if c < 2:
                total = rope(total, 1.0)
            kwin[slot(u, REACH), slab(c)] = total.astype(jnp.bfloat16)

    class Window:
        def __init__(self, u):
            def copy(src, dst_slot, n, dev):
                return rcopy(kwin.at[slot(u, src)], kwin.at[slot(u, dst_slot)],
                             skv.at[u * 4 + n], rkv.at[u * 4 + n], dev)

            self.hop1 = copy(4, 2, 0, ahead)
            self.hop2 = copy(2, 0, 1, ahead)
            self.even1 = copy(4, 3, 2, partner)
            self.even2 = copy(2, 1, 3, partner)
            self.odd1 = copy(2, 3, 2, partner)
            self.odd2 = copy(0, 1, 3, partner)

        def first(self):
            self.hop1.start()

            @pl.when(xl == 0)
            def _():
                self.even1.start()

        def second(self):
            self.hop1.wait_recv()
            self.hop2.start()

            @pl.when(xl == 0)
            def _():
                self.even2.start()

            @pl.when(xl == 1)
            def _():
                self.odd1.start()

        def third(self):
            self.hop2.wait_recv()

            @pl.when(xl == 1)
            def _():
                self.odd2.start()

        def last(self):
            self.even1.wait_recv()
            self.even2.wait_recv()

        def sent(self):
            for copy in (self.hop1, self.hop2, self.even1, self.even2):
                copy.wait_send()

    inv_root = 1.0 / math.sqrt(HEAD)
    steps = Q_PER_KV // PAIR

    def attend(h, first, last):
        u, c = h // 2, h % 2
        window = slice(u * WIN, (u + 1) * WIN)
        keys = kwin[window, slab(c)]
        vals = kwin[window, slab(2 + c)]
        keys_t = keys.T

        def heads(g, carry):
            width = PAIR * TOK
            qrow = rows((h * Q_PER_KV + g * PAIR) * TOK, width)
            scores = dot(keys, qs[qrow, :], NT) * inv_root + wide(bias[...], width)
            top_score = jnp.max(scores, axis=0, keepdims=True)
            expd = jnp.exp(scores - top_score)
            probs = expd * (1.0 / jnp.sum(expd, axis=0, keepdims=True))
            low = probs.astype(jnp.bfloat16)
            pgrad = dot(vals, dos[qrow, :], NT)
            delta = jnp.sum(low.astype(jnp.float32) * pgrad, axis=0, keepdims=True)
            sgrad = (probs * (pgrad - delta)).astype(jnp.bfloat16)
            pcol = cols(g * width, width)
            pt[:, pcol] = low
            dst[:, pcol] = sgrad
            dqt = dot(keys_t, sgrad) * inv_root
            for n in range(PAIR):
                head = (h * Q_PER_KV + g * PAIR + n) * HEAD
                dq[:, cols(head, HEAD)] = dqt[:, slab(n)].T.astype(jnp.bfloat16)
            return carry

        lax.fori_loop(first, last, heads, 0)
        if last == steps:
            hrow = slab(h, Q_PER_KV * TOK)
            tb[window, slab(2 + c)] = dot(pt[...], dos[hrow, :]).astype(jnp.bfloat16)
            tb[window, slab(c)] = (dot(dst[...], qs[hrow, :]) * inv_root).astype(jnp.bfloat16)

    class Terms:
        def __init__(self, u):
            def copy(src, n, dev):
                return rcopy(tb.at[slot(u, src)], ra.at[slab(u * 4 + n)],
                             sb.at[u * 4 + n], rb.at[u * 4 + n], dev)

            self.u = u
            self.a = copy(3, 0, partner)
            self.b = copy(1, 1, partner)
            self.c = copy(0, 2, back)
            self.d = copy(2, 3, back)

        def fold(self, s, n):
            at = slot(self.u, s)
            tb[at, :] = (tb[at, :].astype(jnp.float32)
                         + ra[slab(self.u * 4 + n), :].astype(jnp.float32)).astype(jnp.bfloat16)

        def first(self):
            @pl.when(xl == 0)
            def _():
                self.c.start()

            self.b.start()
            self.a.start()

        def second(self):
            self.b.wait_recv()

            @pl.when(xl == 1)
            def _():
                self.fold(0, 1)
                self.c.start()

            self.a.wait_recv()

            @pl.when(xl == 1)
            def _():
                self.fold(2, 0)

            @pl.when(xl == 0)
            def _():
                self.fold(2, 1)
                self.fold(4, 0)

        def third(self):
            self.c.wait_recv()
            self.fold(2, 2)
            self.d.start()

        def last(self):
            u = self.u
            self.d.wait_recv()
            for c in range(4):
                total = (tb[slot(u, REACH), slab(c)].astype(jnp.float32)
                         + ra[slab(u * 4 + 3), slab(c)].astype(jnp.float32))
                if c < 2:
                    total = rope(total, -1.0)
                gall[half_slab(u, 0), slab(c)] = total.astype(jnp.bfloat16)
            gathers[u].first()

        def sent(self):
            for copy in (self.a, self.b, self.c, self.d):
                copy.wait_send()

    class Gather:
        def __init__(self, u):
            def copy(src, dst_slot, n, dev):
                return rcopy(gall.at[half_slab(u, src)], gall.at[half_slab(u, dst_slot)],
                             sga.at[u * F + n], rga.at[u * F + dst_slot], dev)

            mates = range(2, F, 2)
            self.column = [copy(0, k, k, f_up(k)) for k in mates]
            self.even_side = copy(0, 1, 7, f_up(1))
            self.odd_side = copy(0, 7, 7, f_up(7))
            self.even_on = [copy(7, k - 1, k - 1, f_up(k)) for k in mates]
            self.odd_on = [copy(1, k + 1, k - 1, f_up(k)) for k in mates]
            self.into = [copy(0, k, 0, f_up(k)) for k in range(1, F)]

        def first(self):
            @pl.when(xl == 0)
            def _():
                self.even_side.start()

            @pl.when(xl == 1)
            def _():
                self.odd_side.start()

            for member in self.column:
                member.start()

        def second(self):
            @pl.when(xl == 0)
            def _():
                self.into[6].wait_recv()
                for member in self.even_on:
                    member.start()

            @pl.when(xl == 1)
            def _():
                self.into[0].wait_recv()
                for member in self.odd_on:
                    member.start()

        def arrived(self, k):
            if 1 < k < 7:
                self.into[k - 1].wait_recv()
            else:
                @pl.when(xl == (0 if k == 1 else 1))
                def _():
                    self.into[k - 1].wait_recv()

        def sent(self):
            for member in self.column + [self.even_side] + self.even_on:
                member.wait_send()

    windows = [Window(0), Window(1)]
    terms = [Terms(0), Terms(1)]
    gathers = [Gather(0), Gather(1)]
    own_block(0)
    windows[0].first()
    pltpu.make_async_copy(qs, qs, lsem.at[3]).wait()
    pltpu.make_async_copy(dos, dos, lsem.at[4]).wait()
    windows[0].second()
    windows[0].third()
    windows[0].last()
    attend(0, 0, steps // 2)
    own_block(1)
    windows[1].first()
    attend(0, steps // 2, steps)
    windows[1].second()
    attend(1, 0, steps // 2)
    windows[1].third()
    attend(1, steps // 2, steps)
    terms[0].first()
    windows[1].last()
    attend(2, 0, steps)
    terms[0].second()
    attend(3, 0, steps // 2)
    terms[0].third()
    attend(3, steps // 2, steps)
    terms[1].first()
    out_q = pltpu.make_async_copy(dq, o_q.at[0], osem.at[0])
    out_q.start()
    terms[0].last()
    terms[1].second()
    gathers[0].second()
    terms[1].third()
    terms[1].last()

    dots = jnp.zeros((TOK, 128), jnp.float32)
    for u in range(2):
        for c in range(4):
            dots = dots + (gall[half_slab(u, 0), slab(c)].astype(jnp.float32)
                           * proj[:, slab(u * 4 + c)])
    rinv_own = rown[...]
    mean = jnp.sum(dots, axis=1, keepdims=True) * (1.0 / D)
    bb[...] = rinv_own * rinv_own * mean

    gacc[...] = jnp.zeros_like(gacc)

    def h_copy(k):
        return rcopy(hgs.at[slab(k)], sgr.at[slab(k)], sh.at[k], rh.at[k], f_down(k))

    for place, k in enumerate(ORDER):
        if k > 0:
            if place == 1:
                gathers[1].second()
            gathers[0].arrived(k)
            gathers[1].arrived(k)
        hg = (dot(gall[half_slab(0, k), :], wr[:, 0:KVW], NT)
              + dot(gall[half_slab(1, k), :], wr[:, KVW:], NT))
        scaled = (hg * gain_row).astype(jnp.bfloat16)
        if k > 0:
            hgs[slab(k), :] = scaled
            h_copy(k).start()
        else:
            sgr[slab(k), :] = scaled
        prod = hg * slab_x(k) * wide(inv_rms(k), SLAB)
        part = prod[0:8, :]
        for n in range(1, TOK // 8):
            part = part + prod[slab(n, 8), :]
        gacc[...] = gacc[...] + part

    gterm = jnp.broadcast_to(jnp.sum(gacc[...], axis=0, keepdims=True), (8, SLAB))
    for k in range(T):
        gs[slab(k, 8), :] = gterm[:, slab(k, ROWS)]

    def gs_copy(k):
        return rcopy(gs.at[slab(k, 8)], grecv.at[slab(k, 8)], sgs.at[k], rgs.at[k], t_down(k))

    def ws_copy(k):
        return rcopy(ws.at[slab(k, ROWS)], wrecv.at[slab(k, ROWS)], sws.at[k], rws.at[k],
                     t_down(k))

    def weight_term(k):
        for u in range(2):
            term = dot(ht[slab(k, ROWS), :], gall[slab(u, SLAB), :])
            if k == 0:
                wown[:, slab(u, KVW)] = term
            else:
                ws[slab(k, ROWS), slab(u, KVW)] = term.astype(jnp.bfloat16)
        if k > 0:
            ws_copy(k).start()
            gs_copy(k).start()

    @pl.when(p == 3)
    def _():
        pltpu.make_async_copy(cin, cin, lsem.at[5]).wait()

    def c_copy(n):
        part = slab(n, T)
        return rcopy(cout.at[part], cin.at[part], src_.at[n], rrc.at[n], ((p + 3) % 4, i))

    for place, n in enumerate(ORDER):
        if n > 0:
            h_copy(n).wait_recv()

        @pl.when(p < 3)
        def _():
            c_copy(n).wait_recv()

        a = wide(rown[...], ROWS)
        b = wide(bb[...], ROWS)
        for m in range(T):
            branch = (sgr[slab(n), slab(m, ROWS)].astype(jnp.float32) * a
                      - xs[n * T + m].astype(jnp.float32) * b)
            cout[n * T + m] = (cin[n * T + m].astype(jnp.float32) + branch).astype(jnp.bfloat16)

        @pl.when(p > 0)
        def _():
            c_copy(n).start()

        for m in range(T):
            pltpu.make_async_copy(
                cout.at[n * T + m], o_in.at[0, :, x_cols(n * T + m)], osem.at[1]).start()
        if place < T:
            weight_term((place + 1) % T)

    for k in range(1, T):
        ws_copy(k).wait_recv()
        gs_copy(k).wait_recv()

    gtotal = gs[0:1, :]
    total = wown[...]
    for k in range(1, T):
        total = total + wrecv[slab(k, ROWS), :].astype(jnp.float32)
        gtotal = gtotal + grecv[k * 8:k * 8 + 1, :]
    wown[...] = total
    o_gain[...] = gtotal
    outs = []
    for u in range(2):
        for which, out in ((0, o_kw), (1, o_vw)):
            outs.append(pltpu.make_async_copy(
                wown.at[:, slab(u * 2 + which, 256)], out.at[0, :, slab(u, 256)],
                osem.at[2 + u * 2 + which]))
            outs[-1].start()

    for k in range(1, F):
        x_copy(k).wait_send()
        r_copy(k).wait_send()
        for u in range(2):
            p_copy(u, k).wait_send()
        h_copy(k).wait_send()
    for k in range(1, T):
        w_copy(k).wait_send()
        g_copy(k).wait_send()
        ws_copy(k).wait_send()
        gs_copy(k).wait_send()
    for member in windows + terms + gathers:
        member.sent()

    @pl.when(p > 0)
    def _():
        for n in range(F):
            c_copy(n).wait_send()

    pltpu.make_async_copy(cout, cout, osem.at[1]).wait()
    for copy in [out_q] + outs:
        copy.wait()


def hand_on(in_in, in_q, in_kw, in_vw, in_gain, o_in, o_q, o_kw, o_vw, o_gain, sem):
    copies = []
    for src, dst, parts in ((in_in, o_in, 4), (in_q, o_q, 2), (in_kw, o_kw, 2), (in_vw, o_vw, 2)):
        size = src.shape[1] // parts
        for n in range(parts):
            part = slice(n * size, (n + 1) * size)
            copies.append(pltpu.make_async_copy(
                src.at[0, part], dst.at[0, part], sem.at[len(copies)]))
    copies.append(pltpu.make_async_copy(in_gain, o_gain, sem.at[len(copies)]))
    for copy in copies:
        copy.start()
    for copy in copies:
        copy.wait()


def on_device(layer_input, queries, out_grad, top_grad, norm_gain, key_weight, value_weight,
              weight_exponents, doc_lengths):
    bf, f32 = jnp.bfloat16, jnp.float32
    vmem = functools.partial(pltpu.VMEM)
    dma = pltpu.SemaphoreType.DMA
    hbm = pl.BlockSpec(memory_space=pl.ANY)
    smem = pl.BlockSpec(memory_space=pltpu.SMEM)
    vm = pl.BlockSpec(memory_space=pltpu.VMEM)
    scratch = [
        vmem((F * T, TOK, ROWS), bf),
        vmem((F * T, TOK, ROWS), bf),
        vmem((ROWS, KVW), bf),
        vmem((ROWS, KVW), bf),
        vmem((SLAB, SLAB), bf),
        vmem((8 * T, ROWS), f32),
        vmem((64, 128), f32),
        vmem((TOK, 128), f32),
        vmem((QW, HEAD), bf),
        vmem((QW, HEAD), bf),
        vmem((F * T, TOK, ROWS), bf),
        vmem((F * T, TOK, ROWS), bf),
        vmem((TOK, 128), f32),
        vmem((TOK, 128), f32),
        vmem((WIN, 128), f32),
        vmem((SLAB, SLAB), bf),
        vmem((SLAB, SLAB), bf),
        vmem((TOK, SLAB), f32),
        vmem((2 * SLAB, KVW), bf),
        vmem((2 * SLAB, KVW), bf),
        vmem((2 * WIN, KVW), bf),
        vmem((WIN, SLAB), bf),
        vmem((WIN, SLAB), bf),
        vmem((2 * WIN, KVW), bf),
        vmem((8 * TOK, KVW), bf),
        vmem((TOK, QW), bf),
        vmem((2 * SLAB, KVW), bf),
        vmem((SLAB, SLAB), bf),
        vmem((SLAB, SLAB), bf),
        vmem((TOK, 128), f32),
        vmem((SLAB, SLAB), bf),
        vmem((SLAB, SLAB), bf),
        vmem((ROWS, SLAB), f32),
        vmem((8 * T, ROWS), f32),
        vmem((8 * T, ROWS), f32),
        vmem((8, SLAB), f32),
        dma((6,)), dma((F,)), dma((F,)), dma((F,)), dma((F,)),
        dma((T,)), dma((T,)), dma((T,)), dma((T,)), dma((2 * F,)), dma((2 * F,)),
        dma((8,)), dma((8,)), dma((8,)), dma((8,)),
        dma((2 * F,)), dma((2 * F,)), dma((F,)), dma((F,)),
        dma((T,)), dma((T,)), dma((T,)), dma((T,)),
        dma((F,)), dma((F,)), dma((6,)), dma((F,)),
    ]
    o_in, o_q, o_kw, o_vw, o_gain = pl.pallas_call(
        kernel,
        out_shape=(
            jax.ShapeDtypeStruct((1, TOK, D), bf),
            jax.ShapeDtypeStruct((1, TOK, QW), bf),
            jax.ShapeDtypeStruct((1, ROWS, KVW), f32),
            jax.ShapeDtypeStruct((1, ROWS, KVW), f32),
            jax.ShapeDtypeStruct((1, ROWS), f32),
        ),
        in_specs=[smem, smem, hbm, hbm, hbm, hbm, vm, hbm, hbm],
        out_specs=(hbm, hbm, hbm, hbm, vm),
        scratch_shapes=scratch,
        compiler_params=pltpu.CompilerParams(
            collective_id=0, has_side_effects=True, vmem_limit_bytes=60 * 1024 * 1024),
    )(weight_exponents, doc_lengths, layer_input, queries, out_grad, top_grad, norm_gain,
      key_weight, value_weight)
    results = (o_in, o_q, o_kw, o_vw, o_gain)
    return pl.pallas_call(
        hand_on,
        out_shape=tuple(jax.ShapeDtypeStruct(r.shape, r.dtype) for r in results),
        in_specs=[hbm] * 5,
        out_specs=(hbm,) * 5,
        scratch_shapes=[dma((11,))],
    )(*results)


def solution(mesh):
    in_specs = (
        P("pipe", "dp", None),
        P("pipe", "dp", None),
        P("pipe", "dp", None),
        P("dp", None),
        P("pipe", "dp"),
        P("pipe", "dp", None),
        P("pipe", "dp", None),
        P("pipe", None, "dp", None),
        P(),
    )
    out_specs = (
        P("pipe", "dp", None),
        P("pipe", "dp", None),
        P("pipe", "dp", None),
        P("pipe", "dp", None),
        P("pipe", "dp"),
    )
    return jax.shard_map(
        on_device, mesh=mesh, in_specs=in_specs, out_specs=out_specs, check_vma=False
    )
```

```python
import functools
import math

import jax
import jax.numpy as jnp
import numpy as np
from jax import lax
from jax.experimental import pallas as pl
from jax.experimental.pallas import tpu as pltpu
from jax.sharding import PartitionSpec as P

D = 8192
KV_HEADS = 4
Q_PER_KV = 8
HEAD = 128
TOK = 128
REACH = 4
KVW = 512
QW = 4096
ROWS = 256
THETA = 500000.0
EPS = 1e-05
MASKED = -1e30

F = 8
T = 4
SLAB = 1024
WIN = (REACH + 1) * TOK
PAIR = 4
PARTS = 4
ORDER = (0, 1, 2, 3, 4, 5, 6, 7)

MESH = pl.DeviceIdType.MESH
NT = (((1,), (1,)), ((), ()))
NN = (((1,), (0,)), ((), ()))


def rows(start, size):
    return pl.ds(pl.multiple_of(start, size), size)


def cols(start, size):
    return pl.ds(pl.multiple_of(start, size), size)


def dot(a, b, dims=NN):
    return lax.dot_general(a, b, dims, preferred_element_type=jnp.float32)


def wide(col, width):
    return jnp.concatenate([col] * (width // col.shape[1]), axis=1)


def kernel(
    exps, docs, x, q, do, top, gain, kw, vw,
    o_in, o_q, o_kw, o_vw, o_gain,
    xs, xr, kwv, vwv, wr, gr, rr, rown, qs, dos, cin, cout, cosb, sinb, bias,
    hbuf, ht, proj, psend, precv, kwin, pt, dst, tb, ra, dq, gall, hgs, sgr, bb,
    ws, wrecv, wown, gs, grecv, gacc,
    lsem, sx, rx, sr, rrs, sw, rw, sg, rg, sp, rp, skv, rkv, sb, rb,
    sga, rga, sh, rh, sws, rws, sgs, rgs, src_, rrc, osem, lx,
):
    p = lax.axis_index("pipe")
    i = lax.axis_index("dp")
    f = i % F
    t = i // F
    xl = i % 2

    def slab(k, size=TOK):
        return slice(k * size, (k + 1) * size)

    def f_up(k):
        return (p, t * F + (f + k) % F)

    def f_down(k):
        return (p, t * F + (f + F - k) % F)

    def t_up(k):
        return (p, (t + k) % T * F + f)

    def t_down(k):
        return (p, (t + T - k) % T * F + f)

    def rcopy(src, dst, ssem, rsem, dev):
        return pltpu.make_async_remote_copy(
            src_ref=src, dst_ref=dst, send_sem=ssem, recv_sem=rsem,
            device_id=dev, device_id_type=MESH)

    def x_cols(n):
        return cols(((t + T - n % T) % T * F + (f + n // T) % F) * ROWS, ROWS)

    barrier = pltpu.get_barrier_semaphore()
    peers = [f_up(k) for k in range(1, F)] + [t_up(k) for k in range(1, T)]
    peers += [(p, (i + 2) % 32), (p, (i + 30) % 32)]
    peers += [((p + 1) % 4, i), ((p + 3) % 4, i)]
    for peer in peers:
        pl.semaphore_signal(barrier, inc=1, device_id=peer, device_id_type=MESH)

    def load_slab(k):
        def load(n, carry):
            pltpu.make_async_copy(
                x.at[0, :, x_cols(k * T + n)], xs.at[k * T + n], lx.at[k]).start()
            return carry

        lax.fori_loop(0, T, load, 0)

    order = list(range(1, F)) + [0]
    load_slab(order[0])
    pltpu.make_async_copy(kw.at[0], kwv, lsem.at[1]).start()
    pltpu.make_async_copy(vw.at[0], vwv, lsem.at[2]).start()
    for k in order[1:]:
        load_slab(k)
    pl.semaphore_wait(barrier, len(peers))

    def x_copy(k):
        return rcopy(xs.at[slab(k, T)], xr.at[slab(k, T)], sx.at[k], rx.at[k], f_up(k))

    def wait_slab(k):
        pltpu.make_async_copy(xs.at[slab(k, T)], xs.at[slab(k, T)], lx.at[k]).wait()

    early = 3
    for k in range(1, early):
        wait_slab(k)
        x_copy(k).start()

    pltpu.make_async_copy(kw.at[0], kwv, lsem.at[1]).wait()
    pltpu.make_async_copy(vw.at[0], vwv, lsem.at[2]).wait()
    for rblock in range(2):
        for cblock in range(4):
            for which, wv in ((0, kwv), (1, vwv)):
                block = wv[slab(rblock), slab(cblock)].astype(jnp.float32)
                power = exps[0, which, rblock, cblock]
                place = cblock // 2 * 4 + which * 2 + cblock % 2
                scaled = block * jnp.where(power > 0, 2.0, jnp.where(power < 0, 0.5, 1.0))
                wr[slab(rblock), slab(place)] = scaled.astype(jnp.bfloat16)
    gr[0:8, :] = jnp.broadcast_to(gain[...].astype(jnp.float32), (8, ROWS))

    def w_copy(k):
        return rcopy(wr.at[0:ROWS], wr.at[slab(k, ROWS)], sw.at[k], rw.at[k], t_up(k))

    def g_copy(k):
        return rcopy(gr.at[0:8], gr.at[slab(k, 8)], sg.at[k], rg.at[k], t_up(k))

    for k in range(1, T):
        g_copy(k).start()
        w_copy(k).start()

    for k in range(early, F):
        wait_slab(k)
    wait_slab(0)

    def add_squares(n, acc):
        part = xs[n].astype(jnp.float32)
        part = part * part
        for c in range(ROWS // 128):
            acc = acc + part[:, slab(c)]
        return acc

    squares = lax.fori_loop(0, F * T, add_squares, jnp.zeros((TOK, 128), jnp.float32))
    mean_sq = jnp.sum(squares, axis=1, keepdims=True) * (1.0 / D)
    rinv = jnp.broadcast_to(1.0 / jnp.sqrt(mean_sq + EPS), (TOK, 128))
    rown[...] = rinv
    rr[0:8, :] = rinv.T[0:8, :]

    def r_copy(k):
        return rcopy(rr.at[0:8], rr.at[slab(k, 8)], sr.at[k], rrs.at[k], f_up(k))

    for k in range(1, F):
        r_copy(k).start()
    for k in range(early, F):
        x_copy(k).start()
    xr[0:T] = xs[0:T]

    def load_q(n, carry):
        pltpu.make_async_copy(
            q.at[0, :, cols(n * HEAD, HEAD)], qs.at[rows(n * TOK, TOK)], lsem.at[3]).start()
        pltpu.make_async_copy(
            do.at[0, :, cols(n * HEAD, HEAD)], dos.at[rows(n * TOK, TOK)], lsem.at[4]).start()
        return carry

    lax.fori_loop(0, KV_HEADS * Q_PER_KV, load_q, 0)

    @pl.when(p == 3)
    def _():
        def load_top(n, carry):
            pltpu.make_async_copy(top.at[:, x_cols(n)], cin.at[n], lsem.at[5]).start()
            return carry

        lax.fori_loop(0, F * T, load_top, 0)

    tok_col = i * TOK + lax.broadcasted_iota(jnp.int32, (TOK, 128), 0)
    tok_row = i * TOK + lax.broadcasted_iota(jnp.int32, (8, 128), 1)

    def scan_docs(n, carry):
        start, scol, srow = carry
        scol = jnp.where(start <= tok_col, start, scol)
        srow = jnp.where(start <= tok_row, start, srow)
        return start + docs[n], scol, srow

    _, scol, srow = lax.fori_loop(
        0, 64, scan_docs,
        (jnp.int32(0), jnp.zeros((TOK, 128), jnp.int32), jnp.zeros((8, 128), jnp.int32)))
    lane = lax.broadcasted_iota(jnp.int32, (TOK, 128), 1)
    freq = jnp.ones((TOK, 128), jnp.float32)
    for bit in range(6):
        power = float(np.float64(THETA) ** (-(2.0 * 2 ** bit / HEAD)))
        freq = jnp.where((lane & (1 << bit)) != 0, freq * power, freq)
    angle = (tok_col - scol).astype(jnp.float32) * freq
    sine = jnp.sin(angle)
    cosb[...] = jnp.cos(angle)
    sinb[...] = jnp.where(lane < 64, -sine, sine)
    key_index = (i - REACH) * TOK + lax.broadcasted_iota(jnp.int32, (WIN, 128), 0)
    seen = (key_index >= srow[0:1, :]) & (key_index <= tok_row[0:1, :])
    bias[...] = jnp.where(seen, 0.0, MASKED)

    for k in range(1, T):
        w_copy(k).wait_recv()
        g_copy(k).wait_recv()

    def inv_rms(k):
        return jnp.broadcast_to(rr[k * 8:k * 8 + 1, :], (TOK, 128)).T

    def slab_x(k):
        return jnp.concatenate(
            [xr[k * T + n].astype(jnp.float32) for n in range(T)], axis=1)

    gain_row = jnp.concatenate([gr[n * 8:n * 8 + 1, :] for n in range(T)], axis=1)

    def half_slab(u, k):
        return slab(u * F + k)

    def p_copy(u, k):
        return rcopy(psend.at[half_slab(u, k)], precv.at[half_slab(u, k)],
                     sp.at[u * F + k], rp.at[u * F + k], f_down(k))

    for k in range(F):
        if k > 0:
            x_copy(k).wait_recv()
            r_copy(k).wait_recv()
        hidden = (slab_x(k) * wide(inv_rms(k), SLAB) * gain_row).astype(jnp.bfloat16)
        hbuf[slab(k), :] = hidden
        part = dot(hidden, wr[...]).astype(jnp.bfloat16)
        for u in range(2):
            target = psend if k > 0 else precv
            target[half_slab(u, k), :] = part[:, slab(u, KVW)]
        if k > 0:
            p_copy(0, k).start()
    for k in range(1, F):
        p_copy(1, k).start()

    for k in range(F):
        ht[:, slab(k)] = hbuf[slab(k), :].T

    def rope(block, sign):
        return block * cosb[...] + pltpu.roll(block, 64, 1) * (sinb[...] * sign)

    partner = (p, i + 1 - 2 * xl)
    ahead = (p, (i + 2) % 32)
    back = (p, (i + 30) % 32)

    def slot(u, s):
        return slab(u * (REACH + 1) + s)

    def own_block(u):
        for k in range(1, F):
            p_copy(u, k).wait_recv()
        for c in range(4):
            total = precv[half_slab(u, 0), slab(c)].astype(jnp.float32)
            for k in range(1, F):
                total = total + precv[half_slab(u, k), slab(c)].astype(jnp.float32)
            proj[:, slab(u * 4 + c)] = total
            if c < 2:
                total = rope(total, 1.0)
            kwin[slot(u, REACH), slab(c)] = total.astype(jnp.bfloat16)

    class Window:
        def __init__(self, u):
            def copy(src, dst_slot, n, dev):
                return rcopy(kwin.at[slot(u, src)], kwin.at[slot(u, dst_slot)],
                             skv.at[u * 4 + n], rkv.at[u * 4 + n], dev)

            self.hop1 = copy(4, 2, 0, ahead)
            self.hop2 = copy(2, 0, 1, ahead)
            self.even1 = copy(4, 3, 2, partner)
            self.even2 = copy(2, 1, 3, partner)
            self.odd1 = copy(2, 3, 2, partner)
            self.odd2 = copy(0, 1, 3, partner)

        def first(self):
            self.hop1.start()

            @pl.when(xl == 0)
            def _():
                self.even1.start()

        def second(self):
            self.hop1.wait_recv()
            self.hop2.start()

            @pl.when(xl == 0)
            def _():
                self.even2.start()

            @pl.when(xl == 1)
            def _():
                self.odd1.start()

        def third(self):
            self.hop2.wait_recv()

            @pl.when(xl == 1)
            def _():
                self.odd2.start()

        def last(self):
            self.even1.wait_recv()
            self.even2.wait_recv()

        def sent(self):
            for copy in (self.hop1, self.hop2, self.even1, self.even2):
                copy.wait_send()

    inv_root = 1.0 / math.sqrt(HEAD)
    steps = Q_PER_KV // PAIR

    def attend(h, first, last):
        u, c = h // 2, h % 2
        window = slice(u * WIN, (u + 1) * WIN)
        keys = kwin[window, slab(c)]
        vals = kwin[window, slab(2 + c)]
        keys_t = keys.T

        def heads(g, carry):
            width = PAIR * TOK
            qrow = rows((h * Q_PER_KV + g * PAIR) * TOK, width)
            scores = dot(keys, qs[qrow, :], NT) * inv_root + wide(bias[...], width)
            top_score = jnp.max(scores, axis=0, keepdims=True)
            expd = jnp.exp(scores - top_score)
            probs = expd * (1.0 / jnp.sum(expd, axis=0, keepdims=True))
            low = probs.astype(jnp.bfloat16)
            pgrad = dot(vals, dos[qrow, :], NT)
            delta = jnp.sum(low.astype(jnp.float32) * pgrad, axis=0, keepdims=True)
            sgrad = (probs * (pgrad - delta)).astype(jnp.bfloat16)
            pcol = cols(g * width, width)
            pt[:, pcol] = low
            dst[:, pcol] = sgrad
            dqt = dot(keys_t, sgrad) * inv_root
            for n in range(PAIR):
                head = (h * Q_PER_KV + g * PAIR + n) * HEAD
                dq[:, cols(head, HEAD)] = dqt[:, slab(n)].T.astype(jnp.bfloat16)
            return carry

        lax.fori_loop(first, last, heads, 0)
        if last == steps:
            hrow = slab(h, Q_PER_KV * TOK)
            tb[window, slab(2 + c)] = dot(pt[...], dos[hrow, :]).astype(jnp.bfloat16)
            tb[window, slab(c)] = (dot(dst[...], qs[hrow, :]) * inv_root).astype(jnp.bfloat16)

    class Terms:
        def __init__(self, u):
            def copy(src, n, dev):
                return rcopy(tb.at[slot(u, src)], ra.at[slab(u * 4 + n)],
                             sb.at[u * 4 + n], rb.at[u * 4 + n], dev)

            self.u = u
            self.a = copy(3, 0, partner)
            self.b = copy(1, 1, partner)
            self.c = copy(0, 2, back)
            self.d = copy(2, 3, back)

        def fold(self, s, n):
            at = slot(self.u, s)
            tb[at, :] = (tb[at, :].astype(jnp.float32)
                         + ra[slab(self.u * 4 + n), :].astype(jnp.float32)).astype(jnp.bfloat16)

        def first(self):
            @pl.when(xl == 0)
            def _():
                self.c.start()

            self.b.start()
            self.a.start()

        def second(self):
            self.b.wait_recv()

            @pl.when(xl == 1)
            def _():
                self.fold(0, 1)
                self.c.start()

            self.a.wait_recv()

            @pl.when(xl == 1)
            def _():
                self.fold(2, 0)

            @pl.when(xl == 0)
            def _():
                self.fold(2, 1)
                self.fold(4, 0)

        def third(self):
            self.c.wait_recv()
            self.fold(2, 2)
            self.d.start()

        def last(self):
            u = self.u
            self.d.wait_recv()
            for c in range(4):
                total = (tb[slot(u, REACH), slab(c)].astype(jnp.float32)
                         + ra[slab(u * 4 + 3), slab(c)].astype(jnp.float32))
                if c < 2:
                    total = rope(total, -1.0)
                gall[half_slab(u, 0), slab(c)] = total.astype(jnp.bfloat16)
            gathers[u].first()

        def sent(self):
            for copy in (self.a, self.b, self.c, self.d):
                copy.wait_send()

    class Gather:
        def __init__(self, u):
            self.copies = [rcopy(gall.at[half_slab(u, 0)], gall.at[half_slab(u, k)],
                                 sga.at[u * F + k], rga.at[u * F + k], f_up(k))
                           for k in range(1, F)]

        def first(self):
            for copy in self.copies:
                copy.start()

        def arrived(self, k):
            self.copies[k - 1].wait_recv()

        def sent(self):
            for copy in self.copies:
                copy.wait_send()

    windows = [Window(0), Window(1)]
    terms = [Terms(0), Terms(1)]
    gathers = [Gather(0), Gather(1)]
    own_block(0)
    windows[0].first()
    pltpu.make_async_copy(qs, qs, lsem.at[3]).wait()
    pltpu.make_async_copy(dos, dos, lsem.at[4]).wait()
    windows[0].second()
    windows[0].third()
    own_block(1)
    windows[1].first()
    windows[0].last()
    attend(0, 0, steps // 2)
    windows[1].second()
    attend(0, steps // 2, steps)
    attend(1, 0, steps // 2)
    windows[1].third()
    attend(1, steps // 2, steps)
    terms[0].first()
    windows[1].last()
    attend(2, 0, steps)
    terms[0].second()
    attend(3, 0, steps // 2)
    terms[0].third()
    attend(3, steps // 2, steps)
    terms[1].first()
    out_q = pltpu.make_async_copy(dq, o_q.at[0], osem.at[0])
    out_q.start()
    terms[0].last()
    terms[1].second()
    terms[1].third()
    terms[1].last()

    dots = jnp.zeros((TOK, 128), jnp.float32)
    for u in range(2):
        for c in range(4):
            dots = dots + (gall[half_slab(u, 0), slab(c)].astype(jnp.float32)
                           * proj[:, slab(u * 4 + c)])
    rinv_own = rown[...]
    mean = jnp.sum(dots, axis=1, keepdims=True) * (1.0 / D)
    bb[...] = rinv_own * rinv_own * mean

    gacc[...] = jnp.zeros_like(gacc)

    def h_copy(k):
        return rcopy(hgs.at[slab(k)], sgr.at[slab(k)], sh.at[k], rh.at[k], f_down(k))

    for place, k in enumerate(ORDER):
        if k > 0:
            gathers[0].arrived(k)
            gathers[1].arrived(k)
        hg = (dot(gall[half_slab(0, k), :], wr[:, 0:KVW], NT)
              + dot(gall[half_slab(1, k), :], wr[:, KVW:], NT))
        scaled = (hg * gain_row).astype(jnp.bfloat16)
        if k > 0:
            hgs[slab(k), :] = scaled
            h_copy(k).start()
        else:
            sgr[slab(k), :] = scaled
        prod = hg * slab_x(k) * wide(inv_rms(k), SLAB)
        part = prod[0:8, :]
        for n in range(1, TOK // 8):
            part = part + prod[slab(n, 8), :]
        gacc[...] = gacc[...] + part

    gterm = jnp.broadcast_to(jnp.sum(gacc[...], axis=0, keepdims=True), (8, SLAB))
    for k in range(T):
        gs[slab(k, 8), :] = gterm[:, slab(k, ROWS)]

    def gs_copy(k):
        return rcopy(gs.at[slab(k, 8)], grecv.at[slab(k, 8)], sgs.at[k], rgs.at[k], t_down(k))

    def ws_copy(k):
        return rcopy(ws.at[slab(k, ROWS)], wrecv.at[slab(k, ROWS)], sws.at[k], rws.at[k],
                     t_down(k))

    def weight_term(k):
        for u in range(2):
            term = dot(ht[slab(k, ROWS), :], gall[slab(u, SLAB), :])
            if k == 0:
                wown[:, slab(u, KVW)] = term
            else:
                ws[slab(k, ROWS), slab(u, KVW)] = term.astype(jnp.bfloat16)
        if k > 0:
            ws_copy(k).start()
            gs_copy(k).start()

    @pl.when(p == 3)
    def _():
        pltpu.make_async_copy(cin, cin, lsem.at[5]).wait()

    def c_copy(n):
        part = slab(n, T)
        return rcopy(cout.at[part], cin.at[part], src_.at[n], rrc.at[n], ((p + 3) % 4, i))

    for place, n in enumerate(ORDER):
        if n > 0:
            h_copy(n).wait_recv()

        @pl.when(p < 3)
        def _():
            c_copy(n).wait_recv()

        a = wide(rown[...], ROWS)
        b = wide(bb[...], ROWS)
        for m in range(T):
            branch = (sgr[slab(n), slab(m, ROWS)].astype(jnp.float32) * a
                      - xs[n * T + m].astype(jnp.float32) * b)
            cout[n * T + m] = (cin[n * T + m].astype(jnp.float32) + branch).astype(jnp.bfloat16)

        @pl.when(p > 0)
        def _():
            c_copy(n).start()

        for m in range(T):
            pltpu.make_async_copy(
                cout.at[n * T + m], o_in.at[0, :, x_cols(n * T + m)], osem.at[1]).start()
        if place == 0:
            for part in (1, 2, 3, 0):
                weight_term(part)

    for k in range(1, T):
        ws_copy(k).wait_recv()
        gs_copy(k).wait_recv()

    gtotal = gs[0:1, :]
    total = wown[...]
    for k in range(1, T):
        total = total + wrecv[slab(k, ROWS), :].astype(jnp.float32)
        gtotal = gtotal + grecv[k * 8:k * 8 + 1, :]
    wown[...] = total
    o_gain[...] = gtotal
    outs = []
    for u in range(2):
        for which, out in ((0, o_kw), (1, o_vw)):
            outs.append(pltpu.make_async_copy(
                wown.at[:, slab(u * 2 + which, 256)], out.at[0, :, slab(u, 256)],
                osem.at[2 + u * 2 + which]))
            outs[-1].start()

    for k in range(1, F):
        x_copy(k).wait_send()
        r_copy(k).wait_send()
        for u in range(2):
            p_copy(u, k).wait_send()
        h_copy(k).wait_send()
    for k in range(1, T):
        w_copy(k).wait_send()
        g_copy(k).wait_send()
        ws_copy(k).wait_send()
        gs_copy(k).wait_send()
    for member in windows + terms + gathers:
        member.sent()

    @pl.when(p > 0)
    def _():
        for n in range(F):
            c_copy(n).wait_send()

    pltpu.make_async_copy(cout, cout, osem.at[1]).wait()
    for copy in [out_q] + outs:
        copy.wait()


def hand_on(in_in, in_q, in_kw, in_vw, in_gain, o_in, o_q, o_kw, o_vw, o_gain):
    for src, dst in ((in_in, o_in), (in_q, o_q), (in_kw, o_kw), (in_vw, o_vw), (in_gain, o_gain)):
        dst[...] = src[...]


def on_device(layer_input, queries, out_grad, top_grad, norm_gain, key_weight, value_weight,
              weight_exponents, doc_lengths):
    bf, f32 = jnp.bfloat16, jnp.float32
    vmem = functools.partial(pltpu.VMEM)
    dma = pltpu.SemaphoreType.DMA
    hbm = pl.BlockSpec(memory_space=pl.ANY)
    smem = pl.BlockSpec(memory_space=pltpu.SMEM)
    vm = pl.BlockSpec(memory_space=pltpu.VMEM)
    scratch = [
        vmem((F * T, TOK, ROWS), bf),
        vmem((F * T, TOK, ROWS), bf),
        vmem((ROWS, KVW), bf),
        vmem((ROWS, KVW), bf),
        vmem((SLAB, SLAB), bf),
        vmem((8 * T, ROWS), f32),
        vmem((64, 128), f32),
        vmem((TOK, 128), f32),
        vmem((QW, HEAD), bf),
        vmem((QW, HEAD), bf),
        vmem((F * T, TOK, ROWS), bf),
        vmem((F * T, TOK, ROWS), bf),
        vmem((TOK, 128), f32),
        vmem((TOK, 128), f32),
        vmem((WIN, 128), f32),
        vmem((SLAB, SLAB), bf),
        vmem((SLAB, SLAB), bf),
        vmem((TOK, SLAB), f32),
        vmem((2 * SLAB, KVW), bf),
        vmem((2 * SLAB, KVW), bf),
        vmem((2 * WIN, KVW), bf),
        vmem((WIN, SLAB), bf),
        vmem((WIN, SLAB), bf),
        vmem((2 * WIN, KVW), bf),
        vmem((8 * TOK, KVW), bf),
        vmem((TOK, QW), bf),
        vmem((2 * SLAB, KVW), bf),
        vmem((SLAB, SLAB), bf),
        vmem((SLAB, SLAB), bf),
        vmem((TOK, 128), f32),
        vmem((SLAB, SLAB), bf),
        vmem((SLAB, SLAB), bf),
        vmem((ROWS, SLAB), f32),
        vmem((8 * T, ROWS), f32),
        vmem((8 * T, ROWS), f32),
        vmem((8, SLAB), f32),
        dma((6,)), dma((F,)), dma((F,)), dma((F,)), dma((F,)),
        dma((T,)), dma((T,)), dma((T,)), dma((T,)), dma((2 * F,)), dma((2 * F,)),
        dma((8,)), dma((8,)), dma((8,)), dma((8,)),
        dma((2 * F,)), dma((2 * F,)), dma((F,)), dma((F,)),
        dma((T,)), dma((T,)), dma((T,)), dma((T,)),
        dma((F,)), dma((F,)), dma((6,)), dma((F,)),
    ]
    o_in, o_q, o_kw, o_vw, o_gain = pl.pallas_call(
        kernel,
        out_shape=(
            jax.ShapeDtypeStruct((1, TOK, D), bf),
            jax.ShapeDtypeStruct((1, TOK, QW), bf),
            jax.ShapeDtypeStruct((1, ROWS, KVW), f32),
            jax.ShapeDtypeStruct((1, ROWS, KVW), f32),
            jax.ShapeDtypeStruct((1, ROWS), f32),
        ),
        in_specs=[smem, smem, hbm, hbm, hbm, hbm, vm, hbm, hbm],
        out_specs=(hbm, hbm, hbm, hbm, vm),
        scratch_shapes=scratch,
        compiler_params=pltpu.CompilerParams(
            collective_id=0, has_side_effects=True, vmem_limit_bytes=60 * 1024 * 1024),
    )(weight_exponents, doc_lengths, layer_input, queries, out_grad, top_grad, norm_gain,
      key_weight, value_weight)
    results = (o_in, o_q, o_kw, o_vw, o_gain)
    blocks = [pl.BlockSpec((1, r.shape[1] // PARTS, r.shape[2]), lambda n: (0, n, 0))
              for r in results[:4]]
    blocks.append(pl.BlockSpec((1, ROWS), lambda n: (0, 0)))
    return pl.pallas_call(
        hand_on,
        out_shape=tuple(jax.ShapeDtypeStruct(r.shape, r.dtype) for r in results),
        grid=(PARTS,),
        in_specs=blocks,
        out_specs=tuple(blocks),
    )(*results)


def solution(mesh):
    in_specs = (
        P("pipe", "dp", None),
        P("pipe", "dp", None),
        P("pipe", "dp", None),
        P("dp", None),
        P("pipe", "dp"),
        P("pipe", "dp", None),
        P("pipe", "dp", None),
        P("pipe", None, "dp", None),
        P(),
    )
    out_specs = (
        P("pipe", "dp", None),
        P("pipe", "dp", None),
        P("pipe", "dp", None),
        P("pipe", "dp", None),
        P("pipe", "dp"),
    )
    return jax.shard_map(
        on_device, mesh=mesh, in_specs=in_specs, out_specs=out_specs, check_vma=False
    )
```

```python
import functools
import math

import jax
import jax.numpy as jnp
import numpy as np
from jax import lax
from jax.experimental import pallas as pl
from jax.experimental.pallas import tpu as pltpu
from jax.sharding import PartitionSpec as P

D = 8192
KV_HEADS = 4
Q_PER_KV = 8
HEAD = 128
TOK = 128
REACH = 4
KVW = 512
QW = 4096
ROWS = 256
THETA = 500000.0
EPS = 1e-05
MASKED = -1e30

F = 8
T = 4
SLAB = 1024
WIN = (REACH + 1) * TOK
PAIR = 4
PARTS = 4
ORDER = (0, 1, 2, 3, 4, 5, 6, 7)

MESH = pl.DeviceIdType.MESH
NT = (((1,), (1,)), ((), ()))
NN = (((1,), (0,)), ((), ()))


def rows(start, size):
    return pl.ds(pl.multiple_of(start, size), size)


def cols(start, size):
    return pl.ds(pl.multiple_of(start, size), size)


def dot(a, b, dims=NN):
    return lax.dot_general(a, b, dims, preferred_element_type=jnp.float32)


def wide(col, width):
    return jnp.concatenate([col] * (width // col.shape[1]), axis=1)


def kernel(
    exps, docs, x, q, do, top, gain, kw, vw,
    o_in, o_q, o_kw, o_vw, o_gain,
    xs, xr, kwv, vwv, wr, gr, rr, rown, qs, dos, cin, cout, cosb, sinb, bias,
    hbuf, ht, proj, psend, precv, kwin, pt, dst, tb, ra, dq, gall, hgs, sgr, bb,
    ws, wrecv, wown, gs, grecv, gacc,
    lsem, sx, rx, sr, rrs, sw, rw, sg, rg, sp, rp, skv, rkv, sb, rb,
    sga, rga, sh, rh, sws, rws, sgs, rgs, src_, rrc, osem, lx,
):
    p = lax.axis_index("pipe")
    i = lax.axis_index("dp")
    f = i % F
    t = i // F
    xl = i % 2

    def slab(k, size=TOK):
        return slice(k * size, (k + 1) * size)

    def f_up(k):
        return (p, t * F + (f + k) % F)

    def f_down(k):
        return (p, t * F + (f + F - k) % F)

    def t_up(k):
        return (p, (t + k) % T * F + f)

    def t_down(k):
        return (p, (t + T - k) % T * F + f)

    def rcopy(src, dst, ssem, rsem, dev):
        return pltpu.make_async_remote_copy(
            src_ref=src, dst_ref=dst, send_sem=ssem, recv_sem=rsem,
            device_id=dev, device_id_type=MESH)

    def x_cols(n):
        return cols(((t + T - n % T) % T * F + (f + n // T) % F) * ROWS, ROWS)

    barrier = pltpu.get_barrier_semaphore()
    peers = [f_up(k) for k in range(1, F)] + [t_up(k) for k in range(1, T)]
    peers += [(p, (i + 2) % 32), (p, (i + 30) % 32)]
    peers += [((p + 1) % 4, i), ((p + 3) % 4, i)]
    for peer in peers:
        pl.semaphore_signal(barrier, inc=1, device_id=peer, device_id_type=MESH)

    def load_slab(k):
        def load(n, carry):
            pltpu.make_async_copy(
                x.at[0, :, x_cols(k * T + n)], xs.at[k * T + n], lx.at[k]).start()
            return carry

        lax.fori_loop(0, T, load, 0)

    order = list(range(1, F)) + [0]
    load_slab(order[0])
    pltpu.make_async_copy(kw.at[0], kwv, lsem.at[1]).start()
    pltpu.make_async_copy(vw.at[0], vwv, lsem.at[2]).start()
    for k in order[1:]:
        load_slab(k)
    pl.semaphore_wait(barrier, len(peers))

    def x_copy(k):
        return rcopy(xs.at[slab(k, T)], xr.at[slab(k, T)], sx.at[k], rx.at[k], f_up(k))

    def wait_slab(k):
        pltpu.make_async_copy(xs.at[slab(k, T)], xs.at[slab(k, T)], lx.at[k]).wait()

    early = 3
    for k in range(1, early):
        wait_slab(k)
        x_copy(k).start()

    pltpu.make_async_copy(kw.at[0], kwv, lsem.at[1]).wait()
    pltpu.make_async_copy(vw.at[0], vwv, lsem.at[2]).wait()
    for rblock in range(2):
        for cblock in range(4):
            for which, wv in ((0, kwv), (1, vwv)):
                block = wv[slab(rblock), slab(cblock)].astype(jnp.float32)
                power = exps[0, which, rblock, cblock]
                place = cblock // 2 * 4 + which * 2 + cblock % 2
                scaled = block * jnp.where(power > 0, 2.0, jnp.where(power < 0, 0.5, 1.0))
                wr[slab(rblock), slab(place)] = scaled.astype(jnp.bfloat16)
    gr[0:8, :] = jnp.broadcast_to(gain[...].astype(jnp.float32), (8, ROWS))

    def w_copy(k):
        return rcopy(wr.at[0:ROWS], wr.at[slab(k, ROWS)], sw.at[k], rw.at[k], t_up(k))

    def g_copy(k):
        return rcopy(gr.at[0:8], gr.at[slab(k, 8)], sg.at[k], rg.at[k], t_up(k))

    for k in range(1, T):
        g_copy(k).start()
        w_copy(k).start()

    for k in range(early, F):
        wait_slab(k)
    wait_slab(0)

    def add_squares(n, acc):
        part = xs[n].astype(jnp.float32)
        part = part * part
        for c in range(ROWS // 128):
            acc = acc + part[:, slab(c)]
        return acc

    squares = lax.fori_loop(0, F * T, add_squares, jnp.zeros((TOK, 128), jnp.float32))
    mean_sq = jnp.sum(squares, axis=1, keepdims=True) * (1.0 / D)
    rinv = jnp.broadcast_to(1.0 / jnp.sqrt(mean_sq + EPS), (TOK, 128))
    rown[...] = rinv
    rr[0:8, :] = rinv.T[0:8, :]

    def r_copy(k):
        return rcopy(rr.at[0:8], rr.at[slab(k, 8)], sr.at[k], rrs.at[k], f_up(k))

    for k in range(1, F):
        r_copy(k).start()
    for k in range(early, F):
        x_copy(k).start()
    xr[0:T] = xs[0:T]

    def load_q(n, carry):
        pltpu.make_async_copy(
            q.at[0, :, cols(n * HEAD, HEAD)], qs.at[rows(n * TOK, TOK)], lsem.at[3]).start()
        pltpu.make_async_copy(
            do.at[0, :, cols(n * HEAD, HEAD)], dos.at[rows(n * TOK, TOK)], lsem.at[4]).start()
        return carry

    lax.fori_loop(0, KV_HEADS * Q_PER_KV, load_q, 0)

    @pl.when(p == 3)
    def _():
        def load_top(n, carry):
            pltpu.make_async_copy(top.at[:, x_cols(n)], cin.at[n], lsem.at[5]).start()
            return carry

        lax.fori_loop(0, F * T, load_top, 0)

    tok_col = i * TOK + lax.broadcasted_iota(jnp.int32, (TOK, 128), 0)
    tok_row = i * TOK + lax.broadcasted_iota(jnp.int32, (8, 128), 1)

    def scan_docs(n, carry):
        start, scol, srow = carry
        scol = jnp.where(start <= tok_col, start, scol)
        srow = jnp.where(start <= tok_row, start, srow)
        return start + docs[n], scol, srow

    _, scol, srow = lax.fori_loop(
        0, 64, scan_docs,
        (jnp.int32(0), jnp.zeros((TOK, 128), jnp.int32), jnp.zeros((8, 128), jnp.int32)))
    lane = lax.broadcasted_iota(jnp.int32, (TOK, 128), 1)
    freq = jnp.ones((TOK, 128), jnp.float32)
    for bit in range(6):
        power = float(np.float64(THETA) ** (-(2.0 * 2 ** bit / HEAD)))
        freq = jnp.where((lane & (1 << bit)) != 0, freq * power, freq)
    angle = (tok_col - scol).astype(jnp.float32) * freq
    sine = jnp.sin(angle)
    cosb[...] = jnp.cos(angle)
    sinb[...] = jnp.where(lane < 64, -sine, sine)
    key_index = (i - REACH) * TOK + lax.broadcasted_iota(jnp.int32, (WIN, 128), 0)
    seen = (key_index >= srow[0:1, :]) & (key_index <= tok_row[0:1, :])
    bias[...] = jnp.where(seen, 0.0, MASKED)

    for k in range(1, T):
        w_copy(k).wait_recv()
        g_copy(k).wait_recv()

    def inv_rms(k):
        return jnp.broadcast_to(rr[k * 8:k * 8 + 1, :], (TOK, 128)).T

    def slab_x(k):
        return jnp.concatenate(
            [xr[k * T + n].astype(jnp.float32) for n in range(T)], axis=1)

    gain_row = jnp.concatenate([gr[n * 8:n * 8 + 1, :] for n in range(T)], axis=1)

    def half_slab(u, k):
        return slab(u * F + k)

    def p_copy(u, k):
        return rcopy(psend.at[half_slab(u, k)], precv.at[half_slab(u, k)],
                     sp.at[u * F + k], rp.at[u * F + k], f_down(k))

    def product(u, g):
        part = dot(hbuf[slab(g, 2 * TOK), :], wr[:, slab(u, KVW)]).astype(jnp.bfloat16)
        for n in range(2):
            k = 2 * g + n
            target = psend if k > 0 else precv
            target[half_slab(u, k), :] = part[slab(n), :]
            if k > 0:
                p_copy(u, k).start()

    for k in range(F):
        if k > 0:
            x_copy(k).wait_recv()
            r_copy(k).wait_recv()
        hidden = (slab_x(k) * wide(inv_rms(k), SLAB) * gain_row).astype(jnp.bfloat16)
        hbuf[slab(k), :] = hidden
        if k % 2 == 1:
            product(0, k // 2)
    for g in range(F // 2):
        product(1, g)

    for k in range(F):
        ht[:, slab(k)] = hbuf[slab(k), :].T

    def rope(block, sign):
        return block * cosb[...] + pltpu.roll(block, 64, 1) * (sinb[...] * sign)

    partner = (p, i + 1 - 2 * xl)
    ahead = (p, (i + 2) % 32)
    back = (p, (i + 30) % 32)

    def slot(u, s):
        return slab(u * (REACH + 1) + s)

    def own_block(u):
        for k in range(1, F):
            p_copy(u, k).wait_recv()
        for c in range(4):
            total = precv[half_slab(u, 0), slab(c)].astype(jnp.float32)
            for k in range(1, F):
                total = total + precv[half_slab(u, k), slab(c)].astype(jnp.float32)
            proj[:, slab(u * 4 + c)] = total
            if c < 2:
                total = rope(total, 1.0)
            kwin[slot(u, REACH), slab(c)] = total.astype(jnp.bfloat16)

    class Window:
        def __init__(self, u):
            def copy(src, dst_slot, n, dev):
                return rcopy(kwin.at[slot(u, src)], kwin.at[slot(u, dst_slot)],
                             skv.at[u * 4 + n], rkv.at[u * 4 + n], dev)

            self.hop1 = copy(4, 2, 0, ahead)
            self.hop2 = copy(2, 0, 1, ahead)
            self.even1 = copy(4, 3, 2, partner)
            self.even2 = copy(2, 1, 3, partner)
            self.odd1 = copy(2, 3, 2, partner)
            self.odd2 = copy(0, 1, 3, partner)

        def first(self):
            self.hop1.start()

            @pl.when(xl == 0)
            def _():
                self.even1.start()

        def second(self):
            self.hop1.wait_recv()
            self.hop2.start()

            @pl.when(xl == 0)
            def _():
                self.even2.start()

            @pl.when(xl == 1)
            def _():
                self.odd1.start()

        def third(self):
            self.hop2.wait_recv()

            @pl.when(xl == 1)
            def _():
                self.odd2.start()

        def last(self):
            self.even1.wait_recv()
            self.even2.wait_recv()

        def sent(self):
            for copy in (self.hop1, self.hop2, self.even1, self.even2):
                copy.wait_send()

    inv_root = 1.0 / math.sqrt(HEAD)
    steps = Q_PER_KV // PAIR

    def attend(h, first, last):
        u, c = h // 2, h % 2
        window = slice(u * WIN, (u + 1) * WIN)
        keys = kwin[window, slab(c)]
        vals = kwin[window, slab(2 + c)]
        keys_t = keys.T

        def heads(g, carry):
            width = PAIR * TOK
            qrow = rows((h * Q_PER_KV + g * PAIR) * TOK, width)
            scores = dot(keys, qs[qrow, :], NT) * inv_root + wide(bias[...], width)
            top_score = jnp.max(scores, axis=0, keepdims=True)
            expd = jnp.exp(scores - top_score)
            probs = expd * (1.0 / jnp.sum(expd, axis=0, keepdims=True))
            low = probs.astype(jnp.bfloat16)
            pgrad = dot(vals, dos[qrow, :], NT)
            delta = jnp.sum(low.astype(jnp.float32) * pgrad, axis=0, keepdims=True)
            sgrad = (probs * (pgrad - delta)).astype(jnp.bfloat16)
            pcol = cols(g * width, width)
            pt[:, pcol] = low
            dst[:, pcol] = sgrad
            dqt = dot(keys_t, sgrad) * inv_root
            for n in range(PAIR):
                head = (h * Q_PER_KV + g * PAIR + n) * HEAD
                dq[:, cols(head, HEAD)] = dqt[:, slab(n)].T.astype(jnp.bfloat16)
            return carry

        lax.fori_loop(first, last, heads, 0)
        if last == steps:
            hrow = slab(h, Q_PER_KV * TOK)
            tb[window, slab(2 + c)] = dot(pt[...], dos[hrow, :]).astype(jnp.bfloat16)
            tb[window, slab(c)] = (dot(dst[...], qs[hrow, :]) * inv_root).astype(jnp.bfloat16)

    class Terms:
        def __init__(self, u):
            def copy(src, n, dev):
                return rcopy(tb.at[slot(u, src)], ra.at[slab(u * 4 + n)],
                             sb.at[u * 4 + n], rb.at[u * 4 + n], dev)

            self.u = u
            self.a = copy(3, 0, partner)
            self.b = copy(1, 1, partner)
            self.c = copy(0, 2, back)
            self.d = copy(2, 3, back)

        def fold(self, s, n):
            at = slot(self.u, s)
            tb[at, :] = (tb[at, :].astype(jnp.float32)
                         + ra[slab(self.u * 4 + n), :].astype(jnp.float32)).astype(jnp.bfloat16)

        def first(self):
            @pl.when(xl == 0)
            def _():
                self.c.start()

            self.b.start()
            self.a.start()

        def second(self):
            self.b.wait_recv()

            @pl.when(xl == 1)
            def _():
                self.fold(0, 1)
                self.c.start()

            self.a.wait_recv()

            @pl.when(xl == 1)
            def _():
                self.fold(2, 0)

            @pl.when(xl == 0)
            def _():
                self.fold(2, 1)
                self.fold(4, 0)

        def third(self):
            self.c.wait_recv()
            self.fold(2, 2)
            self.d.start()

        def last(self):
            u = self.u
            self.d.wait_recv()
            for c in range(4):
                total = (tb[slot(u, REACH), slab(c)].astype(jnp.float32)
                         + ra[slab(u * 4 + 3), slab(c)].astype(jnp.float32))
                if c < 2:
                    total = rope(total, -1.0)
                gall[half_slab(u, 0), slab(c)] = total.astype(jnp.bfloat16)
            gathers[u].first()

        def sent(self):
            for copy in (self.a, self.b, self.c, self.d):
                copy.wait_send()

    class Gather:
        def __init__(self, u):
            self.copies = [rcopy(gall.at[half_slab(u, 0)], gall.at[half_slab(u, k)],
                                 sga.at[u * F + k], rga.at[u * F + k], f_up(k))
                           for k in range(1, F)]

        def first(self):
            for copy in self.copies:
                copy.start()

        def arrived(self, k):
            self.copies[k - 1].wait_recv()

        def sent(self):
            for copy in self.copies:
                copy.wait_send()

    windows = [Window(0), Window(1)]
    terms = [Terms(0), Terms(1)]
    gathers = [Gather(0), Gather(1)]
    own_block(0)
    windows[0].first()
    pltpu.make_async_copy(qs, qs, lsem.at[3]).wait()
    pltpu.make_async_copy(dos, dos, lsem.at[4]).wait()
    windows[0].second()
    windows[0].third()
    own_block(1)
    windows[1].first()
    windows[0].last()
    attend(0, 0, steps // 2)
    windows[1].second()
    attend(0, steps // 2, steps)
    attend(1, 0, steps // 2)
    windows[1].third()
    attend(1, steps // 2, steps)
    terms[0].first()
    windows[1].last()
    attend(2, 0, steps)
    terms[0].second()
    attend(3, 0, steps // 2)
    terms[0].third()
    attend(3, steps // 2, steps)
    terms[1].first()
    out_q = pltpu.make_async_copy(dq, o_q.at[0], osem.at[0])
    out_q.start()
    terms[0].last()
    terms[1].second()
    terms[1].third()
    terms[1].last()

    dots = jnp.zeros((TOK, 128), jnp.float32)
    for u in range(2):
        for c in range(4):
            dots = dots + (gall[half_slab(u, 0), slab(c)].astype(jnp.float32)
                           * proj[:, slab(u * 4 + c)])
    rinv_own = rown[...]
    mean = jnp.sum(dots, axis=1, keepdims=True) * (1.0 / D)
    bb[...] = rinv_own * rinv_own * mean

    gacc[...] = jnp.zeros_like(gacc)

    def h_copy(k):
        return rcopy(hgs.at[slab(k)], sgr.at[slab(k)], sh.at[k], rh.at[k], f_down(k))

    for place, k in enumerate(ORDER):
        if k > 0:
            gathers[0].arrived(k)
            gathers[1].arrived(k)
        hg = (dot(gall[half_slab(0, k), :], wr[:, 0:KVW], NT)
              + dot(gall[half_slab(1, k), :], wr[:, KVW:], NT))
        scaled = (hg * gain_row).astype(jnp.bfloat16)
        if k > 0:
            hgs[slab(k), :] = scaled
            h_copy(k).start()
        else:
            sgr[slab(k), :] = scaled
        prod = hg * slab_x(k) * wide(inv_rms(k), SLAB)
        part = prod[0:8, :]
        for n in range(1, TOK // 8):
            part = part + prod[slab(n, 8), :]
        gacc[...] = gacc[...] + part

    gterm = jnp.broadcast_to(jnp.sum(gacc[...], axis=0, keepdims=True), (8, SLAB))
    for k in range(T):
        gs[slab(k, 8), :] = gterm[:, slab(k, ROWS)]

    def gs_copy(k):
        return rcopy(gs.at[slab(k, 8)], grecv.at[slab(k, 8)], sgs.at[k], rgs.at[k], t_down(k))

    def ws_copy(k):
        return rcopy(ws.at[slab(k, ROWS)], wrecv.at[slab(k, ROWS)], sws.at[k], rws.at[k],
                     t_down(k))

    def weight_term(k):
        for u in range(2):
            term = dot(ht[slab(k, ROWS), :], gall[slab(u, SLAB), :])
            if k == 0:
                wown[:, slab(u, KVW)] = term
            else:
                ws[slab(k, ROWS), slab(u, KVW)] = term.astype(jnp.bfloat16)
        if k > 0:
            ws_copy(k).start()
            gs_copy(k).start()

    @pl.when(p == 3)
    def _():
        pltpu.make_async_copy(cin, cin, lsem.at[5]).wait()

    def c_copy(n):
        part = slab(n, T)
        return rcopy(cout.at[part], cin.at[part], src_.at[n], rrc.at[n], ((p + 3) % 4, i))

    for place, n in enumerate(ORDER):
        if n > 0:
            h_copy(n).wait_recv()

        @pl.when(p < 3)
        def _():
            c_copy(n).wait_recv()

        a = wide(rown[...], ROWS)
        b = wide(bb[...], ROWS)
        for m in range(T):
            branch = (sgr[slab(n), slab(m, ROWS)].astype(jnp.float32) * a
                      - xs[n * T + m].astype(jnp.float32) * b)
            cout[n * T + m] = (cin[n * T + m].astype(jnp.float32) + branch).astype(jnp.bfloat16)

        @pl.when(p > 0)
        def _():
            c_copy(n).start()

        for m in range(T):
            pltpu.make_async_copy(
                cout.at[n * T + m], o_in.at[0, :, x_cols(n * T + m)], osem.at[1]).start()
        if place == 0:
            for part in (1, 2, 3, 0):
                weight_term(part)

    for k in range(1, T):
        ws_copy(k).wait_recv()
        gs_copy(k).wait_recv()

    gtotal = gs[0:1, :]
    total = wown[...]
    for k in range(1, T):
        total = total + wrecv[slab(k, ROWS), :].astype(jnp.float32)
        gtotal = gtotal + grecv[k * 8:k * 8 + 1, :]
    wown[...] = total
    o_gain[...] = gtotal
    outs = []
    for u in range(2):
        for which, out in ((0, o_kw), (1, o_vw)):
            outs.append(pltpu.make_async_copy(
                wown.at[:, slab(u * 2 + which, 256)], out.at[0, :, slab(u, 256)],
                osem.at[2 + u * 2 + which]))
            outs[-1].start()

    for k in range(1, F):
        x_copy(k).wait_send()
        r_copy(k).wait_send()
        for u in range(2):
            p_copy(u, k).wait_send()
        h_copy(k).wait_send()
    for k in range(1, T):
        w_copy(k).wait_send()
        g_copy(k).wait_send()
        ws_copy(k).wait_send()
        gs_copy(k).wait_send()
    for member in windows + terms + gathers:
        member.sent()

    @pl.when(p > 0)
    def _():
        for n in range(F):
            c_copy(n).wait_send()

    pltpu.make_async_copy(cout, cout, osem.at[1]).wait()
    for copy in [out_q] + outs:
        copy.wait()


def hand_on(in_in, in_q, in_kw, in_vw, in_gain, o_in, o_q, o_kw, o_vw, o_gain):
    for src, dst in ((in_in, o_in), (in_q, o_q), (in_kw, o_kw), (in_vw, o_vw), (in_gain, o_gain)):
        dst[...] = src[...]


def on_device(layer_input, queries, out_grad, top_grad, norm_gain, key_weight, value_weight,
              weight_exponents, doc_lengths):
    bf, f32 = jnp.bfloat16, jnp.float32
    vmem = functools.partial(pltpu.VMEM)
    dma = pltpu.SemaphoreType.DMA
    hbm = pl.BlockSpec(memory_space=pl.ANY)
    smem = pl.BlockSpec(memory_space=pltpu.SMEM)
    vm = pl.BlockSpec(memory_space=pltpu.VMEM)
    scratch = [
        vmem((F * T, TOK, ROWS), bf),
        vmem((F * T, TOK, ROWS), bf),
        vmem((ROWS, KVW), bf),
        vmem((ROWS, KVW), bf),
        vmem((SLAB, SLAB), bf),
        vmem((8 * T, ROWS), f32),
        vmem((64, 128), f32),
        vmem((TOK, 128), f32),
        vmem((QW, HEAD), bf),
        vmem((QW, HEAD), bf),
        vmem((F * T, TOK, ROWS), bf),
        vmem((F * T, TOK, ROWS), bf),
        vmem((TOK, 128), f32),
        vmem((TOK, 128), f32),
        vmem((WIN, 128), f32),
        vmem((SLAB, SLAB), bf),
        vmem((SLAB, SLAB), bf),
        vmem((TOK, SLAB), f32),
        vmem((2 * SLAB, KVW), bf),
        vmem((2 * SLAB, KVW), bf),
        vmem((2 * WIN, KVW), bf),
        vmem((WIN, SLAB), bf),
        vmem((WIN, SLAB), bf),
        vmem((2 * WIN, KVW), bf),
        vmem((8 * TOK, KVW), bf),
        vmem((TOK, QW), bf),
        vmem((2 * SLAB, KVW), bf),
        vmem((SLAB, SLAB), bf),
        vmem((SLAB, SLAB), bf),
        vmem((TOK, 128), f32),
        vmem((SLAB, SLAB), bf),
        vmem((SLAB, SLAB), bf),
        vmem((ROWS, SLAB), f32),
        vmem((8 * T, ROWS), f32),
        vmem((8 * T, ROWS), f32),
        vmem((8, SLAB), f32),
        dma((6,)), dma((F,)), dma((F,)), dma((F,)), dma((F,)),
        dma((T,)), dma((T,)), dma((T,)), dma((T,)), dma((2 * F,)), dma((2 * F,)),
        dma((8,)), dma((8,)), dma((8,)), dma((8,)),
        dma((2 * F,)), dma((2 * F,)), dma((F,)), dma((F,)),
        dma((T,)), dma((T,)), dma((T,)), dma((T,)),
        dma((F,)), dma((F,)), dma((6,)), dma((F,)),
    ]
    o_in, o_q, o_kw, o_vw, o_gain = pl.pallas_call(
        kernel,
        out_shape=(
            jax.ShapeDtypeStruct((1, TOK, D), bf),
            jax.ShapeDtypeStruct((1, TOK, QW), bf),
            jax.ShapeDtypeStruct((1, ROWS, KVW), f32),
            jax.ShapeDtypeStruct((1, ROWS, KVW), f32),
            jax.ShapeDtypeStruct((1, ROWS), f32),
        ),
        in_specs=[smem, smem, hbm, hbm, hbm, hbm, vm, hbm, hbm],
        out_specs=(hbm, hbm, hbm, hbm, vm),
        scratch_shapes=scratch,
        compiler_params=pltpu.CompilerParams(
            collective_id=0, has_side_effects=True, vmem_limit_bytes=60 * 1024 * 1024),
    )(weight_exponents, doc_lengths, layer_input, queries, out_grad, top_grad, norm_gain,
      key_weight, value_weight)
    results = (o_in, o_q, o_kw, o_vw, o_gain)
    blocks = [pl.BlockSpec((1, r.shape[1] // PARTS, r.shape[2]), lambda n: (0, n, 0))
              for r in results[:4]]
    blocks.append(pl.BlockSpec((1, ROWS), lambda n: (0, 0)))
    return pl.pallas_call(
        hand_on,
        out_shape=tuple(jax.ShapeDtypeStruct(r.shape, r.dtype) for r in results),
        grid=(PARTS,),
        in_specs=blocks,
        out_specs=tuple(blocks),
    )(*results)


def solution(mesh):
    in_specs = (
        P("pipe", "dp", None),
        P("pipe", "dp", None),
        P("pipe", "dp", None),
        P("dp", None),
        P("pipe", "dp"),
        P("pipe", "dp", None),
        P("pipe", "dp", None),
        P("pipe", None, "dp", None),
        P(),
    )
    out_specs = (
        P("pipe", "dp", None),
        P("pipe", "dp", None),
        P("pipe", "dp", None),
        P("pipe", "dp", None),
        P("pipe", "dp"),
    )
    return jax.shard_map(
        on_device, mesh=mesh, in_specs=in_specs, out_specs=out_specs, check_vma=False
    )
```
